32 devices in a mesh: frames: 4 (over y, core), bricks: 8 (over z, x).
Axes of the slice: x: 2, y: 2, z: 4, core: 2. Of those that a mesh axis runs over, the one named last changes fastest.
Arguments:
- positions: float32 [3, 8, 16384], P(None, 'frames', 'bricks'), may hold values from 0 to 1
- counts: int32 [8, 8], P('frames'), may hold values from 1 to 2048, as said below
- kvec_x: int32 [128], replicated, may hold values from 1 to 64
- kvec_y: int32 [128], replicated, may hold values from 1 to 64
- kvec_z: int32 [8], replicated, may hold values from 1 to 64
Outputs:
- spectrum: float32 [128, 128, 8, 128], P('bricks', 'frames')
The draws below stay inside these ranges and needn't reach their ends.
Inputs may be any that keep to these rules, and one draw needn't show every extreme that they name: `counts`: in every frame one brick holds exactly 2048 live atoms; the others hold 1 to 2048.
All inputs are finite; a program needn't handle non-finite values.
Results may differ from the reference program's by a relative error of at most 0.0033.
Values sent between devices are 32-bit elements; how exact they have to be, the bound alone decides.
No kernel may reach another device: no remote copies, remote signals or barrier semaphores. Data moves between devices by JAX's collectives and lax.ppermute only.
A program may use at most 64 MiB of HBM per device.

```python
import math
import jax
import jax.numpy as jnp
from jax import lax

KX = 128
KY = 128
KZ = 8
NW = 128
CAP = 2048
SERIES = 8
ATOMS = 16384
N_BRICKS = 8


def draw_counts(key, part):
    filled = jax.random.randint(key, (SERIES, N_BRICKS), 1, CAP + 1)
    chosen = jax.random.randint(jax.random.fold_in(key, 7), (SERIES,), 0, N_BRICKS)
    bricks_row = jnp.arange(N_BRICKS, dtype=jnp.int32)
    return jnp.where(bricks_row[None, :] == chosen[:, None], CAP, filled).astype(jnp.int32)


def plant(array, stream_key, low, largest):
    spot = [jax.random.randint(jax.random.fold_in(stream_key, axis), (), 0, length) for axis, length in enumerate(array.shape)]
    longest = array.shape.index(max(array.shape))
    neighbour = spot[:longest] + [(spot[longest] + 1) % array.shape[longest]] + spot[longest + 1:]
    return array.at[tuple(spot)].set(low).at[tuple(neighbour)].set(largest)


def level_of(stream_key, dims, split, least, high):
    level, own = 1.0, jax.random.fold_in(stream_key, 6)
    for position, blocks in split:
        draws = jnp.exp(jax.random.uniform(jax.random.fold_in(own, position), (blocks,), jnp.float32, least / len(split), high / len(split)))
        level = level * jnp.repeat(draws, dims[position] // blocks).reshape([-1 if axis == position else 1 for axis in range(len(dims))])
    return level


def setup_inputs(seed: int = 0) -> dict:
    splits = jax.random.split(jax.random.key(seed), 6)
    return {
        "positions": jnp.clip(1.0 * jax.random.uniform(splits[0], (3, SERIES, ATOMS), jnp.float32) ** level_of(splits[0], (3, SERIES, ATOMS), ((1, 4), (2, 8)), -0.2, 0.2), 0.0, 1.0),
        "counts": draw_counts(jax.random.fold_in(splits[5], 71), 0),
        "kvec_x": plant(jax.random.randint(splits[2], (KX,), 1, 65), jax.random.fold_in(splits[2], 1), 1, 64).astype(jnp.int32),
        "kvec_y": plant(jax.random.randint(splits[3], (KY,), 1, 65), jax.random.fold_in(splits[3], 1), 1, 64).astype(jnp.int32),
        "kvec_z": plant(jax.random.randint(splits[4], (KZ,), 1, 65), jax.random.fold_in(splits[4], 1), 1, 64).astype(jnp.int32),
    }


def block_factors(coords, valid, wave_x, wave_y, wave_z):
    two_pi = 2.0 * math.pi
    length = coords.shape[1]
    ang_x = two_pi * (coords[0][:, None] * wave_x.astype(jnp.float32)[None, :])
    ang_z = two_pi * (coords[2][:, None] * wave_z.astype(jnp.float32)[None, :])
    cos_x, sin_x = jnp.cos(ang_x), jnp.sin(ang_x)
    cos_z, sin_z = jnp.cos(ang_z), jnp.sin(ang_z)
    a_real = cos_x[:, :, None] * cos_z[:, None, :] - sin_x[:, :, None] * sin_z[:, None, :]
    a_imag = -(sin_x[:, :, None] * cos_z[:, None, :] + cos_x[:, :, None] * sin_z[:, None, :])
    left = (jnp.concatenate([a_real.reshape(length, -1), a_imag.reshape(length, -1)], axis=1) * valid[:, None]).astype(jnp.bfloat16)
    ang_y = two_pi * (coords[1][:, None] * wave_y.astype(jnp.float32)[None, :])
    right = jnp.concatenate([jnp.cos(ang_y), -jnp.sin(ang_y)], axis=1).astype(jnp.bfloat16)
    return left, right


def combine(accum):
    half = accum.shape[-2] // 2
    cols = accum.shape[-1] // 2
    real_part = accum[..., :half, :cols] - accum[..., half:, cols:]
    imag_part = accum[..., :half, cols:] + accum[..., half:, :cols]
    return jnp.stack([real_part, imag_part], axis=-2)


def reference(positions, counts, kvec_x, kvec_y, kvec_z):
    frames_total = positions.shape[1]
    pos_frames = jnp.transpose(positions, (1, 0, 2))

    def frame_density(item):
        coords_all, count_row = item

        def brick_step(brick, accum):
            start = (brick * CAP).astype(jnp.int32)
            coords = lax.dynamic_slice(coords_all, (jnp.int32(0), start), (3, CAP))
            limit = lax.dynamic_index_in_dim(count_row, brick, 0, keepdims=False)
            valid = (jnp.arange(CAP, dtype=jnp.int32) < limit).astype(jnp.float32)
            left, right = block_factors(coords, valid, kvec_x, kvec_y, kvec_z)
            return accum + jnp.dot(left.astype(jnp.float32).T, right.astype(jnp.float32), precision=lax.Precision.HIGHEST)

        accum = lax.fori_loop(0, N_BRICKS, brick_step, jnp.zeros((2 * KX * KZ, 2 * KY), jnp.float32))
        return jnp.transpose(combine(accum).reshape(KX, KZ, 2, KY), (0, 2, 1, 3))

    density = lax.map(frame_density, (pos_frames, counts))
    times = jnp.arange(frames_total, dtype=jnp.int32)
    freqs = jnp.arange(NW, dtype=jnp.int32)
    angle = 2.0 * math.pi * ((times[:, None] * freqs[None, :]) % NW).astype(jnp.float32) / NW
    window = 0.5 - 0.5 * jnp.cos(2.0 * math.pi * (times.astype(jnp.float32) + 0.5) / frames_total)
    cos_table = window[:, None] * jnp.cos(angle)
    sin_table = window[:, None] * jnp.sin(angle)
    real_part = density[:, :, 0]
    imag_part = density[:, :, 1]
    high = lax.Precision.HIGHEST
    re_x = jnp.einsum('tazb,tm->abzm', real_part, cos_table, precision=high) + jnp.einsum('tazb,tm->abzm', imag_part, sin_table, precision=high)
    im_x = jnp.einsum('tazb,tm->abzm', imag_part, cos_table, precision=high) - jnp.einsum('tazb,tm->abzm', real_part, sin_table, precision=high)
    norm_total = CAP * N_BRICKS * jnp.sum(window * window)
    return (re_x * re_x + im_x * im_x) / norm_total
```

```python
import functools
import math

import jax
import jax.numpy as jnp
import numpy as np
from jax import lax
from jax.experimental import pallas as pl
from jax.experimental.pallas import tpu as pltpu
from jax.sharding import PartitionSpec as P

NW = 128
KMAX = 64
LANES = 128
UNIT = 2

def _fit(fun, degree):
    nodes = 0.125 * (1.0 + np.cos(np.pi * (np.arange(64) + 0.5) / 64))
    series = np.polynomial.chebyshev.Chebyshev.fit(nodes, fun(np.sqrt(nodes)), degree, domain=[0.0, 0.25])
    return [float(c) for c in series.convert(kind=np.polynomial.Polynomial).coef]


COS_C = _fit(lambda f: math.sqrt(2.0) * np.cos(np.pi * f), 4)
SIN_C = _fit(lambda f: math.sqrt(2.0) * np.sin(np.pi * f) / f, 4)


def _poly(coefs, u):
    acc = coefs[-1] * u + coefs[-2]
    for c in coefs[-3::-1]:
        acc = acc * u + c
    return acc


def cis(turns):
    f = turns - jnp.round(turns)
    u = f * f
    half_c = _poly(COS_C, u)
    half_s = _poly(SIN_C, u) * f
    return 1.0 - half_s * half_s, half_s * half_c


def density_kernel(frames, n_x, n_z, dests, counts_ref, me_ref, *refs):
    n_pos = len(frames[1])
    held = frames[1]
    frames_here = frames[0]
    pos_refs = refs[:n_pos]
    kb_ref, ky_ref = refs[n_pos : n_pos + 2]
    outs = refs[n_pos + 2 : n_pos + 2 + dests]
    prod_ref = refs[n_pos + 2 + dests]
    rows = n_x * n_z
    capacity = pos_refs[0].shape[-1]
    step = UNIT * LANES
    me = me_ref[0]
    lane = lax.broadcasted_iota(jnp.int32, (n_z, LANES), 1)

    def factors(pos_ref, shard, frame, offset, count):
        where = pl.ds(pl.multiple_of(offset, LANES), LANES)
        x = pos_ref[shard, 0, pl.ds(frame, 1), where]
        y = pos_ref[shard, 1, pl.ds(frame, 1), where]
        z = pos_ref[shard, 2, pl.ds(frame, 1), where]
        cx, sx = cis(kb_ref[0:n_x, :] * x)
        cz, sz = cis(kb_ref[n_x : n_x + n_z, :] * z)
        cy, sy = cis(kb_ref[n_x + n_z : n_x + n_z + 16, :] * y)
        live = lane + offset < count
        cz = jnp.where(live, cz, 0.0)
        sz = jnp.where(live, sz, 0.0)
        re, im = [], []
        for i in range(n_x):
            a, b = cx[i : i + 1], sx[i : i + 1]
            re.append(a * cz - b * sz)
            im.append(b * cz + a * sz)
        left = jnp.concatenate(re + im, axis=0).astype(jnp.bfloat16)
        ce, se = cy[0:8], sy[0:8]
        re, im = [ce], [se]
        for i in range(8, 15):
            a, b = cy[i : i + 1], sy[i : i + 1]
            re.append(a * ce - b * se)
            im.append(b * ce + a * se)
        right = jnp.concatenate(re + im, axis=0).astype(jnp.bfloat16)
        return left, right

    width = dests * (ky_ref.shape[1] // dests)
    share = width // dests
    ks = lax.broadcasted_iota(jnp.int32, (KMAX, width), 0) + 1
    hot = jnp.where(ks == ky_ref[...], 1.0, 0.0).astype(jnp.bfloat16)
    none = jnp.zeros_like(hot)
    hot = jnp.concatenate(
        [jnp.concatenate([hot, none], axis=1), jnp.concatenate([none, hot], axis=1)], axis=0
    )
    hot = jnp.concatenate([hot, hot, hot], axis=0)

    for frame in range(frames_here):
        prod_ref[...] = jnp.zeros_like(prod_ref)
        for pos_ref, ids in zip(pos_refs, held):
            for shard, distance in enumerate(ids):
                count = counts_ref[frame, me ^ distance]

                def body(block, carry, pos_ref=pos_ref, shard=shard, count=count):
                    parts = [
                        factors(pos_ref, shard, frame, block * step + g * LANES, count)
                        for g in range(UNIT)
                    ]
                    left = jnp.concatenate([p[0] for p in parts], axis=1)
                    right = jnp.concatenate([p[1] for p in parts], axis=1)
                    prod_ref[...] += lax.dot_general(
                        left, right, (((1,), (1,)), ((), ())), preferred_element_type=jnp.float32
                    )
                    return carry

                lax.fori_loop(0, (count + step - 1) // step, body, 0)
        top = prod_ref[0:rows, :]
        low = pltpu.roll(prod_ref[rows : 2 * rows, :], KMAX, 1)
        first = lax.broadcasted_iota(jnp.int32, (rows, 2 * KMAX), 1) < KMAX
        terms = jnp.where(first, top - low, -(top + low))
        hi = terms.astype(jnp.bfloat16)
        rest = terms - hi.astype(jnp.float32)
        mid = rest.astype(jnp.bfloat16)
        tail = (rest - mid.astype(jnp.float32)).astype(jnp.bfloat16)
        split = jnp.concatenate([hi, mid, tail], axis=1)
        picked = lax.dot_general(
            hot, split, (((0,), (1,)), ((), ())), preferred_element_type=jnp.float32
        )
        for part in range(2):
            for dest in range(dests):
                at = part * width + dest * share
                to = (frame * 2 + part) * share
                outs[dest][to : to + share, :] = picked[at : at + share, :]


def spectrum_kernel(groups, share, chunk, n_x, n_z, me_ref, *refs):
    srcs = refs[:groups]
    table_ref, out_ref, all_ref = refs[groups:]
    block = srcs[0].shape[0]
    terms = groups * block // share

    @pl.when(pl.program_id(0) == 0)
    def _():
        for distance in range(groups):
            at = pl.multiple_of((me_ref[0] ^ distance) * block, block)
            all_ref[pl.ds(at, block), :] = srcs[distance][...]

    base = pl.program_id(0) * chunk
    for pair in range(chunk // 2):
        j = base + 2 * pair
        x = jnp.concatenate(
            [all_ref[pl.ds(j + q, terms, stride=share), :] for q in range(2)], axis=0
        )
        hi = x.astype(jnp.bfloat16)
        lo = (x - hi.astype(jnp.float32)).astype(jnp.bfloat16)
        y = lax.dot_general(
            jnp.concatenate([hi, hi, lo], axis=0),
            table_ref[...],
            (((0,), (0,)), ((), ())),
            preferred_element_type=jnp.float32,
        )
        for q in range(2):
            re = y[:, 2 * q * NW : (2 * q + 1) * NW]
            im = y[:, (2 * q + 1) * NW : (2 * q + 2) * NW]
            out_ref[:, 2 * pair + q] = (re * re + im * im).reshape(n_x, n_z, NW)


def dft_table(frames_total, atoms):
    times = jnp.arange(frames_total, dtype=jnp.int32)
    freqs = jnp.arange(NW, dtype=jnp.int32)
    angle = 2.0 * math.pi * (times[:, None] * freqs[None, :] % NW).astype(jnp.float32) / NW
    window = 0.5 - 0.5 * jnp.cos(2.0 * math.pi * (times.astype(jnp.float32) + 0.5) / frames_total)
    scale = lax.rsqrt(atoms * jnp.sum(window * window))
    cw = scale * window[:, None] * jnp.cos(angle)
    sw = scale * window[:, None] * jnp.sin(angle)
    real_row = jnp.concatenate([cw, -sw], axis=1)
    imag_row = jnp.concatenate([sw, cw], axis=1)
    full = jnp.stack([real_row, imag_row], axis=1).reshape(2 * frames_total, 2 * NW)
    none = jnp.zeros_like(full)
    pair = jnp.concatenate(
        [jnp.concatenate([full, none], axis=1), jnp.concatenate([none, full], axis=1)], axis=0
    )
    hi = pair.astype(jnp.bfloat16)
    lo = (pair - hi.astype(jnp.float32)).astype(jnp.bfloat16)
    return jnp.concatenate([hi, lo, hi], axis=0)


def swap(value, axis, size, distance):
    return lax.ppermute(value, axis, [(i, i ^ distance) for i in range(size)])


def per_device(positions, counts, kvec_x, kvec_y, kvec_z):
    groups = lax.axis_size("frames")
    bricks = lax.axis_size("bricks")
    brick = lax.axis_index("bricks")
    group = lax.axis_index("frames")
    frames_here, capacity = positions.shape[1], positions.shape[2]
    n_x, n_z = kvec_x.shape[0] // bricks, kvec_z.shape[0]
    rows = n_x * n_z
    share = kvec_y.shape[0] // groups

    own_x = lax.dynamic_slice(kvec_x, (brick * n_x,), (n_x,))
    waves = jnp.concatenate([own_x, kvec_z, jnp.arange(1, 9), jnp.arange(8, 72, 8)]).astype(jnp.float32)
    kb = jnp.broadcast_to(waves[:, None], (waves.shape[0], LANES))
    order = group ^ jnp.arange(groups, dtype=jnp.int32)
    ky = kvec_y.reshape(groups, share)[order].reshape(1, groups * share)
    table = dft_table(frames_here * groups, capacity * bricks)

    held, ids = positions[None], [0]
    distance = bricks // 2
    while distance:
        got = swap(held, "bricks", bricks, distance)
        held = jnp.concatenate([held, got], axis=0)
        ids = ids + [i ^ distance for i in ids]
        distance //= 2

    vmem = pl.BlockSpec(memory_space=pltpu.VMEM)
    smem = pl.BlockSpec(memory_space=pltpu.SMEM)
    block = frames_here * 2 * share
    sends = pl.pallas_call(
        functools.partial(density_kernel, (frames_here, [ids]), n_x, n_z, groups),
        out_shape=[jax.ShapeDtypeStruct((block, rows), jnp.float32)] * groups,
        in_specs=[smem, smem] + [vmem] * 3,
        out_specs=[vmem] * groups,
        scratch_shapes=[pltpu.VMEM((2 * rows, 2 * KMAX), jnp.float32)],
        name="density",
    )(counts, brick.reshape(1), held, kb, ky)
    got = [sends[0]] + [swap(sends[d], "frames", groups, d) for d in range(1, groups)]

    chunk = min(8, share)
    const = lambda shape: pl.BlockSpec(shape, lambda c: (0, 0))
    return pl.pallas_call(
        functools.partial(spectrum_kernel, groups, share, chunk, n_x, n_z),
        out_shape=jax.ShapeDtypeStruct((n_x, share, n_z, NW), jnp.float32),
        grid=(share // chunk,),
        in_specs=[smem] + [const((block, rows))] * groups + [const(table.shape)],
        out_specs=pl.BlockSpec((n_x, chunk, n_z, NW), lambda c: (0, c, 0, 0)),
        scratch_shapes=[pltpu.VMEM((groups * block, rows), jnp.float32)],
        name="spectrum",
    )(group.reshape(1), *got, table)


def solution(mesh):
    return jax.shard_map(
        per_device,
        mesh=mesh,
        in_specs=(P(None, "frames", "bricks"), P("frames", None), P(), P(), P()),
        out_specs=P("bricks", "frames", None, None),
        check_vma=False,
    )
```

```python
import functools
import math

import jax
import jax.numpy as jnp
import numpy as np
from jax import lax
from jax.experimental import pallas as pl
from jax.experimental.pallas import tpu as pltpu
from jax.sharding import PartitionSpec as P

NW = 128
KMAX = 64
LANES = 128
UNIT = 4
BIG = 4

def _fit(fun, degree):
    nodes = 0.125 * (1.0 + np.cos(np.pi * (np.arange(64) + 0.5) / 64))
    series = np.polynomial.chebyshev.Chebyshev.fit(nodes, fun(np.sqrt(nodes)), degree, domain=[0.0, 0.25])
    return [float(c) for c in series.convert(kind=np.polynomial.Polynomial).coef]


COS_C = _fit(lambda f: math.sqrt(2.0) * np.cos(np.pi * f), 4)
SIN_C = _fit(lambda f: math.sqrt(2.0) * np.sin(np.pi * f) / f, 4)


def _poly(coefs, u):
    acc = coefs[-1] * u + coefs[-2]
    for c in coefs[-3::-1]:
        acc = acc * u + c
    return acc


def cis(turns):
    f = turns - jnp.round(turns)
    u = f * f
    half_c = _poly(COS_C, u)
    half_s = _poly(SIN_C, u) * f
    return 1.0 - half_s * half_s, half_s * half_c


def density_kernel(ids, first, last, groups, n_x, n_z, share, *refs):
    counts_ref, kx_ref, ky_ref, kz_ref, pos_ref = refs[:5]
    prod_in = None if first else refs[5]
    outs = refs[5:-3] if first else refs[6:-3]
    kb_ref, left_ref, right_ref = refs[-3:]
    rows = n_x * n_z
    n_shards, _, frames_here, capacity = pos_ref.shape
    brick = lax.axis_index("bricks")
    group = lax.axis_index("frames")
    lane = lax.broadcasted_iota(jnp.int32, (n_z, LANES), 1)

    for row in range(n_x + n_z + 16):
        if row < n_x:
            k = kx_ref[brick * n_x + row].astype(jnp.float32)
        elif row < n_x + n_z:
            k = kz_ref[row - n_x].astype(jnp.float32)
        else:
            q = row - n_x - n_z
            k = float(q + 1 if q < 8 else 8 * (q - 7))
        kb_ref[row : row + 1, :] = jnp.full((1, LANES), k, jnp.float32)

    for frame in range(frames_here):
        counts = [counts_ref[frame, brick ^ d] for d in ids]
        starts = [jnp.int32(0)]
        for count in counts:
            starts.append(starts[-1] + (count + LANES - 1) // LANES)

        def build(item, frame=frame, counts=counts, starts=starts):
            shard, start, count = jnp.int32(0), starts[0], counts[0]
            for s in range(1, n_shards):
                later = item >= starts[s]
                shard = jnp.where(later, s, shard)
                start = jnp.where(later, starts[s], start)
                count = jnp.where(later, counts[s], count)
            offset = (item - start) * LANES
            where = pl.ds(pl.multiple_of(jnp.minimum(offset, capacity - LANES), LANES), LANES)
            x = pos_ref[shard, 0, pl.ds(frame, 1), where]
            y = pos_ref[shard, 1, pl.ds(frame, 1), where]
            z = pos_ref[shard, 2, pl.ds(frame, 1), where]
            cx, sx = cis(kb_ref[0:n_x, :] * x)
            cz, sz = cis(kb_ref[n_x : n_x + n_z, :] * z)
            cy, sy = cis(kb_ref[n_x + n_z : n_x + n_z + 16, :] * y)
            live = lane + offset < count
            cz = jnp.where(live, cz, 0.0)
            sz = jnp.where(live, sz, 0.0)
            to = pl.ds(pl.multiple_of(item * LANES, LANES), LANES)
            for i in range(0, n_x, 2):
                re, im = [], []
                for q in (i, i + 1):
                    a, b = cx[q : q + 1], sx[q : q + 1]
                    re.append(a * cz - b * sz)
                    im.append(b * cz + a * sz)
                at = i * n_z
                left_ref[at : at + 2 * n_z, to] = jnp.concatenate(re, axis=0).astype(jnp.bfloat16)
                at += rows
                left_ref[at : at + 2 * n_z, to] = jnp.concatenate(im, axis=0).astype(jnp.bfloat16)
            ce, se = cy[0:8], sy[0:8]
            re, im = [ce], [se]
            for q in range(8, 15):
                a, b = cy[q : q + 1], sy[q : q + 1]
                re.append(a * ce - b * se)
                im.append(b * ce + a * se)
            for q in range(0, 8, 2):
                right_ref[8 * q : 8 * q + 16, to] = jnp.concatenate(re[q : q + 2], axis=0).astype(jnp.bfloat16)
                right_ref[KMAX + 8 * q : KMAX + 8 * q + 16, to] = jnp.concatenate(im[q : q + 2], axis=0).astype(jnp.bfloat16)

        def build_unit(unit, carry, build=build):
            for g in range(UNIT):
                build(unit * UNIT + g)
            return carry

        units = (starts[-1] + UNIT - 1) // UNIT
        lax.fori_loop(0, units, build_unit, 0)
        prod_ref = outs[0].at[frame] if not last else outs[-1].at[frame]
        prod_ref[...] = jnp.zeros(prod_ref.shape, jnp.float32) if first else prod_in[frame]

        def multiply(width):
            def step(base):
                where = pl.ds(pl.multiple_of(base, UNIT * LANES), width)
                prod_ref[...] += lax.dot_general(
                    left_ref[:, where],
                    right_ref[:, where],
                    (((1,), (1,)), ((), ())),
                    preferred_element_type=jnp.float32,
                )

            return step

        wide, narrow = multiply(BIG * UNIT * LANES), multiply(UNIT * LANES)
        full = units // BIG

        def wide_step(i, carry, wide=wide):
            wide(i * (BIG * UNIT * LANES))
            return carry

        def narrow_step(i, carry, narrow=narrow):
            narrow(i * (UNIT * LANES))
            return carry

        lax.fori_loop(0, full, wide_step, 0)
        lax.fori_loop(full * BIG, units, narrow_step, 0)
    if last:
        send_own_rows(outs, group, groups, rows, share, frames_here, ky_ref)


def send_own_rows(outs, group, groups, rows, share, frames_here, ky_ref):
    hot_ref, prods = outs[-2], outs[-1]
    column = lax.broadcasted_iota(jnp.int32, (1, 2 * KMAX), 1) + 1
    width = groups * share
    for dest in range(groups):
        base = (group ^ dest) * share
        for j in range(share):
            k = ky_ref[base + j]
            at = dest * share + j
            hot_ref[at : at + 1, :] = jnp.where(column == k, 1.0, 0.0)
            hot_ref[width + at : width + at + 1, :] = jnp.where(column == k + KMAX, 1.0, 0.0)
    hot = hot_ref[...].astype(jnp.bfloat16)
    hot = jnp.concatenate([hot, hot, hot], axis=1)
    first_half = lax.broadcasted_iota(jnp.int32, (rows, 2 * KMAX), 1) < KMAX
    for frame in range(frames_here):
        top = prods[frame, 0:rows, :]
        low = pltpu.roll(prods[frame, rows : 2 * rows, :], KMAX, 1)
        terms = jnp.where(first_half, top - low, -(top + low))
        hi = terms.astype(jnp.bfloat16)
        rest = terms - hi.astype(jnp.float32)
        mid = rest.astype(jnp.bfloat16)
        tail = (rest - mid.astype(jnp.float32)).astype(jnp.bfloat16)
        split = jnp.concatenate([hi, mid, tail], axis=1)
        picked = lax.dot_general(
            hot, split, (((1,), (1,)), ((), ())), preferred_element_type=jnp.float32
        )
        for part in range(2):
            for dest in range(groups):
                at = part * width + dest * share
                to = (frame * 2 + part) * share
                outs[dest][to : to + share, :] = picked[at : at + share, :]


def dft_table(table_ref, frames_total, atoms):
    weights = [0.5 - 0.5 * math.cos(2.0 * math.pi * (t + 0.5) / frames_total) for t in range(frames_total)]
    scale = 1.0 / math.sqrt(atoms * sum(w * w for w in weights))
    shape = (2 * frames_total, NW)
    row = lax.broadcasted_iota(jnp.int32, shape, 0)
    time = row // 2
    real = row % 2 == 0
    freq = lax.broadcasted_iota(jnp.int32, shape, 1)
    window = 0.5 - 0.5 * cis((time.astype(jnp.float32) + 0.5) / frames_total)[0]
    c, s = cis((time * freq % NW).astype(jnp.float32) / NW)
    cw, sw = scale * window * c, scale * window * s
    full = jnp.concatenate([jnp.where(real, cw, sw), jnp.where(real, -sw, cw)], axis=1)
    hi = full.astype(jnp.bfloat16)
    lo = (full - hi.astype(jnp.float32)).astype(jnp.bfloat16)
    none = jnp.zeros_like(hi)
    size = 2 * frames_total
    for split, part in enumerate((hi, lo, hi)):
        at = split * 2 * size
        table_ref[at : at + size, :] = jnp.concatenate([part, none], axis=1)
        table_ref[at + size : at + 2 * size, :] = jnp.concatenate([none, part], axis=1)


def spectrum_kernel(groups, share, chunk, n_x, n_z, frames_total, atoms, *refs):
    srcs = refs[:groups]
    out_ref, all_ref, table_ref = refs[groups:]
    block = srcs[0].shape[0]
    terms = groups * block // share

    @pl.when(pl.program_id(0) == 0)
    def _():
        for distance in range(groups):
            at = pl.multiple_of((lax.axis_index("frames") ^ distance) * block, block)
            all_ref[pl.ds(at, block), :] = srcs[distance][...]
        dft_table(table_ref, frames_total, atoms)

    base = pl.program_id(0) * chunk
    for pair in range(chunk // 2):
        j = base + 2 * pair
        x = jnp.concatenate(
            [all_ref[pl.ds(j + q, terms, stride=share), :] for q in range(2)], axis=0
        )
        hi = x.astype(jnp.bfloat16)
        lo = (x - hi.astype(jnp.float32)).astype(jnp.bfloat16)
        y = lax.dot_general(
            jnp.concatenate([hi, hi, lo], axis=0),
            table_ref[...],
            (((0,), (0,)), ((), ())),
            preferred_element_type=jnp.float32,
        )
        for q in range(2):
            re = y[:, 2 * q * NW : (2 * q + 1) * NW]
            im = y[:, (2 * q + 1) * NW : (2 * q + 2) * NW]
            out_ref[:, 2 * pair + q] = (re * re + im * im).reshape(n_x, n_z, NW)


def swap(value, axis, size, distance):
    return lax.ppermute(value, axis, [(i, i ^ distance) for i in range(size)])


def per_device(positions, counts, kvec_x, kvec_y, kvec_z):
    groups = lax.axis_size("frames")
    bricks = lax.axis_size("bricks")
    frames_here, capacity = positions.shape[1], positions.shape[2]
    n_x, n_z = kvec_x.shape[0] // bricks, kvec_z.shape[0]
    rows = n_x * n_z
    share = kvec_y.shape[0] // groups
    block = frames_here * 2 * share
    vmem = pl.BlockSpec(memory_space=pltpu.VMEM)
    smem = pl.BlockSpec(memory_space=pltpu.SMEM)
    prods_shape = (frames_here, 2 * rows, 2 * KMAX)

    def density(shards, ids, prods, last):
        first = prods is None
        lanes = -(-len(ids) * capacity // (BIG * UNIT * LANES)) * BIG * UNIT * LANES
        scratch = [
            pltpu.VMEM((n_x + n_z + 16, LANES), jnp.float32),
            pltpu.VMEM((2 * rows, lanes), jnp.bfloat16),
            pltpu.VMEM((2 * KMAX, lanes), jnp.bfloat16),
        ]
        if last:
            out_shape = [jax.ShapeDtypeStruct((block, rows), jnp.float32)] * groups
            scratch = [
                pltpu.VMEM((2 * groups * share, 2 * KMAX), jnp.float32),
                pltpu.VMEM(prods_shape, jnp.float32),
            ] + scratch
        else:
            out_shape = [jax.ShapeDtypeStruct(prods_shape, jnp.float32)]
        atoms = frames_here * len(ids) * capacity
        return pl.pallas_call(
            functools.partial(density_kernel, ids, first, last, groups, n_x, n_z, share),
            out_shape=out_shape,
            in_specs=[smem] * 4 + [vmem] * (1 if first else 2),
            out_specs=[vmem] * len(out_shape),
            scratch_shapes=scratch,
            cost_estimate=pl.CostEstimate(
                flops=atoms * rows * KMAX * 8, bytes_accessed=atoms * 12, transcendentals=0
            ),
            compiler_params=pltpu.CompilerParams(vmem_limit_bytes=48 << 20),
            name="density",
        )(counts, kvec_x, kvec_y, kvec_z, shards, *([] if first else [prods]))

    held, fresh, ids = positions[None], positions[None], [0]
    new, prods = [0], None
    distance = bricks // 2
    while distance:
        got = swap(held, "bricks", bricks, distance)
        prods = density(fresh, new, prods, False)[0]
        got, prods = lax.optimization_barrier((got, prods))
        new = [i ^ distance for i in ids]
        ids, fresh = ids + new, got
        distance //= 2
        if distance:
            held = jnp.concatenate([held, got], axis=0)
    sends = density(fresh, new, prods, True)
    got = [sends[0]] + [swap(sends[d], "frames", groups, d) for d in range(1, groups)]

    chunk = min(8, share)
    frames_total = frames_here * groups
    return pl.pallas_call(
        functools.partial(
            spectrum_kernel, groups, share, chunk, n_x, n_z, frames_total, capacity * bricks
        ),
        out_shape=jax.ShapeDtypeStruct((n_x, share, n_z, NW), jnp.float32),
        grid=(share // chunk,),
        in_specs=[vmem] * groups,
        out_specs=pl.BlockSpec((n_x, chunk, n_z, NW), lambda c: (0, c, 0, 0)),
        scratch_shapes=[
            pltpu.VMEM((groups * block, rows), jnp.float32),
            pltpu.VMEM((12 * frames_total, 4 * NW), jnp.bfloat16),
        ],
        name="spectrum",
    )(*got)


def solution(mesh):
    return jax.shard_map(
        per_device,
        mesh=mesh,
        in_specs=(P(None, "frames", "bricks"), P("frames", None), P(), P(), P()),
        out_specs=P("bricks", "frames", None, None),
        check_vma=False,
    )
```

```python
import functools
import math

import jax
import jax.numpy as jnp
import numpy as np
from jax import lax
from jax.experimental import pallas as pl
from jax.experimental.pallas import tpu as pltpu
from jax.sharding import PartitionSpec as P

NW = 128
KMAX = 64
LANES = 128
UNIT = 4
BIG = 4

def _fit(fun, degree):
    nodes = 0.125 * (1.0 + np.cos(np.pi * (np.arange(64) + 0.5) / 64))
    series = np.polynomial.chebyshev.Chebyshev.fit(nodes, fun(np.sqrt(nodes)), degree, domain=[0.0, 0.25])
    return [float(c) for c in series.convert(kind=np.polynomial.Polynomial).coef]


COS_C = _fit(lambda f: math.sqrt(2.0) * np.cos(np.pi * f), 4)
SIN_C = _fit(lambda f: math.sqrt(2.0) * np.sin(np.pi * f) / f, 4)


def _poly(coefs, u):
    acc = coefs[-1] * u + coefs[-2]
    for c in coefs[-3::-1]:
        acc = acc * u + c
    return acc


def cis(turns):
    f = turns - jnp.round(turns)
    u = f * f
    half_c = _poly(COS_C, u)
    half_s = _poly(SIN_C, u) * f
    return 1.0 - half_s * half_s, half_s * half_c


def density_kernel(ids, first, last, groups, n_x, n_z, share, *refs):
    ints_ref, pos_ref = refs[:2]
    prod_in, kb_ref = (None, refs[3]) if first else refs[2:4]
    outs = refs[2:-2] if first else refs[4:-2]
    left_ref, right_ref = refs[-2:]
    rows = n_x * n_z
    n_shards, _, frames_here, capacity = pos_ref.shape
    bricks = lax.axis_size("bricks")
    brick = lax.axis_index("bricks")
    lane = lax.broadcasted_iota(jnp.int32, (n_z, LANES), 1)
    at_x = frames_here * bricks
    at_z = at_x + n_x * bricks
    at_y = at_z + n_z

    if first:
        for row in range(n_x + n_z + 16):
            if row < n_x:
                k = ints_ref[at_x + brick * n_x + row].astype(jnp.float32)
            elif row < n_x + n_z:
                k = ints_ref[at_z + row - n_x].astype(jnp.float32)
            else:
                q = row - n_x - n_z
                k = float(q + 1 if q < 8 else 8 * (q - 7))
            kb_ref[row : row + 1, :] = jnp.full((1, LANES), k, jnp.float32)

    for frame in range(frames_here):
        counts = [ints_ref[frame * bricks + (brick ^ d)] for d in ids]
        starts = [jnp.int32(0)]
        for count in counts:
            starts.append(starts[-1] + (count + LANES - 1) // LANES)

        def build(item, frame=frame, counts=counts, starts=starts):
            shard, start, count = jnp.int32(0), starts[0], counts[0]
            for s in range(1, n_shards):
                later = item >= starts[s]
                shard = jnp.where(later, s, shard)
                start = jnp.where(later, starts[s], start)
                count = jnp.where(later, counts[s], count)
            offset = (item - start) * LANES
            where = pl.ds(pl.multiple_of(jnp.minimum(offset, capacity - LANES), LANES), LANES)
            x = pos_ref[shard, 0, pl.ds(frame, 1), where]
            y = pos_ref[shard, 1, pl.ds(frame, 1), where]
            z = pos_ref[shard, 2, pl.ds(frame, 1), where]
            cx, sx = cis(kb_ref[0:n_x, :] * x)
            cz, sz = cis(kb_ref[n_x : n_x + n_z, :] * z)
            cy, sy = cis(kb_ref[n_x + n_z : n_x + n_z + 16, :] * y)
            live = lane + offset < count
            cz = jnp.where(live, cz, 0.0)
            sz = jnp.where(live, sz, 0.0)
            to = pl.ds(pl.multiple_of(item * LANES, LANES), LANES)
            for i in range(0, n_x, 2):
                re, im = [], []
                for q in (i, i + 1):
                    a, b = cx[q : q + 1], sx[q : q + 1]
                    re.append(a * cz - b * sz)
                    im.append(b * cz + a * sz)
                at = i * n_z
                left_ref[at : at + 2 * n_z, to] = jnp.concatenate(re, axis=0).astype(jnp.bfloat16)
                at += rows
                left_ref[at : at + 2 * n_z, to] = jnp.concatenate(im, axis=0).astype(jnp.bfloat16)
            ce, se = cy[0:8], sy[0:8]
            re, im = [ce], [se]
            for q in range(8, 15):
                a, b = cy[q : q + 1], sy[q : q + 1]
                re.append(a * ce - b * se)
                im.append(b * ce + a * se)
            for q in range(0, 8, 2):
                right_ref[8 * q : 8 * q + 16, to] = jnp.concatenate(re[q : q + 2], axis=0).astype(jnp.bfloat16)
                right_ref[KMAX + 8 * q : KMAX + 8 * q + 16, to] = jnp.concatenate(im[q : q + 2], axis=0).astype(jnp.bfloat16)

        def build_unit(unit, carry, build=build):
            for g in range(UNIT):
                build(unit * UNIT + g)
            return carry

        units = (starts[-1] + UNIT - 1) // UNIT
        lax.fori_loop(0, units, build_unit, 0)
        prod_ref = outs[0].at[frame] if not last else outs[-1].at[frame]
        prod_ref[...] = jnp.zeros(prod_ref.shape, jnp.float32) if first else prod_in[frame]

        def multiply(width):
            def step(base):
                where = pl.ds(pl.multiple_of(base, UNIT * LANES), width)
                prod_ref[...] += lax.dot_general(
                    left_ref[:, where],
                    right_ref[:, where],
                    (((1,), (1,)), ((), ())),
                    preferred_element_type=jnp.float32,
                )

            return step

        wide = multiply(BIG * UNIT * LANES)
        full = units // BIG

        def wide_step(i, carry, wide=wide):
            wide(i * (BIG * UNIT * LANES))
            return carry

        lax.fori_loop(0, full, wide_step, 0)
        for rest in range(1, BIG):

            @pl.when(units - full * BIG == rest)
            def _(rest=rest, multiply=multiply, full=full):
                multiply(rest * UNIT * LANES)(full * (BIG * UNIT * LANES))

    if last:
        send_own_rows(outs, groups, rows, share, frames_here, ints_ref, at_y)


def send_own_rows(outs, groups, rows, share, frames_here, ints_ref, at_y):
    prods = outs[-1]
    width = groups * share
    group = lax.axis_index("frames")
    column = lax.broadcasted_iota(jnp.int32, (1, width), 1)
    wanted = jnp.zeros((1, width), jnp.int32)
    for dest in range(groups):
        base = at_y + (group ^ dest) * share
        for j in range(share):
            wanted = jnp.where(column == dest * share + j, ints_ref[base + j], wanted)
    ks = lax.broadcasted_iota(jnp.int32, (KMAX, width), 0) + 1
    hot = jnp.where(ks == wanted, 1.0, 0.0).astype(jnp.bfloat16)
    none = jnp.zeros_like(hot)
    hot = jnp.concatenate(
        [jnp.concatenate([hot, none], axis=1), jnp.concatenate([none, hot], axis=1)], axis=0
    )
    hot = jnp.concatenate([hot, hot, hot], axis=0)
    first_half = lax.broadcasted_iota(jnp.int32, (rows, 2 * KMAX), 1) < KMAX
    for frame in range(frames_here):
        top = prods[frame, 0:rows, :]
        low = pltpu.roll(prods[frame, rows : 2 * rows, :], KMAX, 1)
        terms = jnp.where(first_half, top - low, -(top + low))
        hi = terms.astype(jnp.bfloat16)
        rest = terms - hi.astype(jnp.float32)
        mid = rest.astype(jnp.bfloat16)
        tail = (rest - mid.astype(jnp.float32)).astype(jnp.bfloat16)
        split = jnp.concatenate([hi, mid, tail], axis=1)
        picked = lax.dot_general(
            hot, split, (((0,), (1,)), ((), ())), preferred_element_type=jnp.float32
        )
        for part in range(2):
            for dest in range(groups):
                at = part * width + dest * share
                to = (frame * 2 + part) * share
                outs[dest][to : to + share, :] = picked[at : at + share, :]


def dft_table(table_ref, frames_total, atoms):
    weights = [0.5 - 0.5 * math.cos(2.0 * math.pi * (t + 0.5) / frames_total) for t in range(frames_total)]
    scale = 1.0 / math.sqrt(atoms * sum(w * w for w in weights))
    shape = (2 * frames_total, NW)
    row = lax.broadcasted_iota(jnp.int32, shape, 0)
    time = row // 2
    real = row % 2 == 0
    freq = lax.broadcasted_iota(jnp.int32, shape, 1)
    window = 0.5 - 0.5 * cis((time.astype(jnp.float32) + 0.5) / frames_total)[0]
    c, s = cis((time * freq % NW).astype(jnp.float32) / NW)
    cw, sw = scale * window * c, scale * window * s
    full = jnp.concatenate([jnp.where(real, cw, sw), jnp.where(real, -sw, cw)], axis=1)
    hi = full.astype(jnp.bfloat16)
    lo = (full - hi.astype(jnp.float32)).astype(jnp.bfloat16)
    none = jnp.zeros_like(hi)
    size = 2 * frames_total
    for split, part in enumerate((hi, lo, hi)):
        at = split * 2 * size
        table_ref[at : at + size, :] = jnp.concatenate([part, none], axis=1)
        table_ref[at + size : at + 2 * size, :] = jnp.concatenate([none, part], axis=1)


def spectrum_kernel(groups, share, chunk, n_x, n_z, frames_total, atoms, *refs):
    srcs = refs[:groups]
    out_ref, all_ref, table_ref = refs[groups:]
    block = srcs[0].shape[0]
    terms = groups * block // share

    @pl.when(pl.program_id(0) == 0)
    def _():
        for distance in range(groups):
            at = pl.multiple_of((lax.axis_index("frames") ^ distance) * block, block)
            all_ref[pl.ds(at, block), :] = srcs[distance][...]
        dft_table(table_ref, frames_total, atoms)

    base = pl.program_id(0) * chunk
    for pair in range(chunk // 2):
        j = base + 2 * pair
        x = jnp.concatenate(
            [all_ref[pl.ds(j + q, terms, stride=share), :] for q in range(2)], axis=0
        )
        hi = x.astype(jnp.bfloat16)
        lo = (x - hi.astype(jnp.float32)).astype(jnp.bfloat16)
        y = lax.dot_general(
            jnp.concatenate([hi, hi, lo], axis=0),
            table_ref[...],
            (((0,), (0,)), ((), ())),
            preferred_element_type=jnp.float32,
        )
        for q in range(2):
            re = y[:, 2 * q * NW : (2 * q + 1) * NW]
            im = y[:, (2 * q + 1) * NW : (2 * q + 2) * NW]
            out_ref[:, 2 * pair + q] = (re * re + im * im).reshape(n_x, n_z, NW)


def swap(value, axis, size, distance):
    return lax.ppermute(value, axis, [(i, i ^ distance) for i in range(size)])


def per_device(positions, counts, kvec_x, kvec_y, kvec_z):
    groups = lax.axis_size("frames")
    bricks = lax.axis_size("bricks")
    frames_here, capacity = positions.shape[1], positions.shape[2]
    n_x, n_z = kvec_x.shape[0] // bricks, kvec_z.shape[0]
    rows = n_x * n_z
    share = kvec_y.shape[0] // groups
    block = frames_here * 2 * share
    vmem = pl.BlockSpec(memory_space=pltpu.VMEM)
    smem = pl.BlockSpec(memory_space=pltpu.SMEM)
    prods_shape = (frames_here, 2 * rows, 2 * KMAX)
    waves_shape = (n_x + n_z + 16, LANES)
    ints = jnp.concatenate([counts.reshape(-1), kvec_x, kvec_z, kvec_y])

    def density(shards, ids, sums, last):
        first = sums is None
        lanes = -(-len(ids) * capacity // (BIG * UNIT * LANES)) * BIG * UNIT * LANES
        scratch = [
            pltpu.VMEM((2 * rows, lanes), jnp.bfloat16),
            pltpu.VMEM((2 * KMAX, lanes), jnp.bfloat16),
        ]
        if last:
            out_shape = [jax.ShapeDtypeStruct((block, rows), jnp.float32)] * groups
            scratch = [pltpu.VMEM(prods_shape, jnp.float32)] + scratch
        else:
            out_shape = [jax.ShapeDtypeStruct(prods_shape, jnp.float32)]
            if first:
                out_shape.append(jax.ShapeDtypeStruct(waves_shape, jnp.float32))
        atoms = frames_here * len(ids) * capacity
        return pl.pallas_call(
            functools.partial(density_kernel, ids, first, last, groups, n_x, n_z, share),
            out_shape=out_shape,
            in_specs=[smem] + [vmem] * (1 if first else 3),
            out_specs=[vmem] * len(out_shape),
            scratch_shapes=scratch,
            cost_estimate=pl.CostEstimate(
                flops=atoms * rows * KMAX * 8, bytes_accessed=atoms * 12, transcendentals=0
            ),
            compiler_params=pltpu.CompilerParams(vmem_limit_bytes=48 << 20),
            name="density",
        )(ints, shards, *([] if first else sums))

    held, fresh, ids = positions[None], positions[None], [0]
    new, sums, waves = [0], None, None
    distance = bricks // 2
    while distance:
        got = swap(held, "bricks", bricks, distance)
        out = density(fresh, new, sums, False)
        waves = out[1] if sums is None else waves
        got, prods = lax.optimization_barrier((got, out[0]))
        sums = (prods, waves)
        new = [i ^ distance for i in ids]
        ids, fresh = ids + new, got
        distance //= 2
        if distance:
            held = jnp.concatenate([held, got], axis=0)
    sends = density(fresh, new, sums, True)
    got = [sends[0]] + [swap(sends[d], "frames", groups, d) for d in range(1, groups)]

    chunk = min(8, share)
    frames_total = frames_here * groups
    return pl.pallas_call(
        functools.partial(
            spectrum_kernel, groups, share, chunk, n_x, n_z, frames_total, capacity * bricks
        ),
        out_shape=jax.ShapeDtypeStruct((n_x, share, n_z, NW), jnp.float32),
        grid=(share // chunk,),
        in_specs=[vmem] * groups,
        out_specs=pl.BlockSpec((n_x, chunk, n_z, NW), lambda c: (0, c, 0, 0)),
        scratch_shapes=[
            pltpu.VMEM((groups * block, rows), jnp.float32),
            pltpu.VMEM((12 * frames_total, 4 * NW), jnp.bfloat16),
        ],
        compiler_params=pltpu.CompilerParams(vmem_limit_bytes=16 << 20),
        name="spectrum",
    )(*got)


def solution(mesh):
    return jax.shard_map(
        per_device,
        mesh=mesh,
        in_specs=(P(None, "frames", "bricks"), P("frames", None), P(), P(), P()),
        out_specs=P("bricks", "frames", None, None),
        check_vma=False,
    )
```

```python
import functools
import math

import jax
import jax.numpy as jnp
import numpy as np
from jax import lax
from jax.experimental import pallas as pl
from jax.experimental.pallas import tpu as pltpu
from jax.sharding import PartitionSpec as P

NW = 128
KMAX = 64
LANES = 128
UNIT = 4
BIG = 8

def _fit(fun, degree):
    nodes = 0.125 * (1.0 + np.cos(np.pi * (np.arange(64) + 0.5) / 64))
    series = np.polynomial.chebyshev.Chebyshev.fit(nodes, fun(np.sqrt(nodes)), degree, domain=[0.0, 0.25])
    return [float(c) for c in series.convert(kind=np.polynomial.Polynomial).coef]


COS_C = _fit(lambda f: math.sqrt(2.0) * np.cos(np.pi * f), 4)
SIN_C = _fit(lambda f: math.sqrt(2.0) * np.sin(np.pi * f) / f, 4)


def _poly(coefs, u):
    acc = coefs[-1] * u + coefs[-2]
    for c in coefs[-3::-1]:
        acc = acc * u + c
    return acc


def cis(turns):
    f = turns - jnp.round(turns)
    u = f * f
    half_c = _poly(COS_C, u)
    half_s = _poly(SIN_C, u) * f
    return 1.0 - half_s * half_s, half_s * half_c


def density_kernel(ids, first, last, groups, n_x, n_z, share, *refs):
    n_args = 4 if first else 2 if last else 1
    args, refs = refs[:n_args], refs[n_args:]
    left_ref, right_ref, row_ref, arg_sem = refs[-4:]
    refs = refs[:-4]
    if not first:
        (pos_ref, prod_in, kb_ref), refs = refs[:3], refs[3:]
    local = refs[-n_args:]
    outs = refs[:-n_args]
    copies = [
        pltpu.make_async_copy(args[i], local[i], arg_sem.at[i]) for i in range(n_args)
    ]
    for copy in copies:
        copy.start()
    counts_ref = local[0]
    if first:
        pos_ref, kb_ref = local[3], outs[1]
    rows = n_x * n_z
    n_shards, _, frames_here, capacity = pos_ref.shape
    brick = lax.axis_index("bricks")
    lane = lax.broadcasted_iota(jnp.int32, (n_z, LANES), 1)

    copies[0].wait()
    if first:
        kx_ref, kz_ref = local[1:3]
        copies[1].wait()
        copies[2].wait()
        for row in range(n_x + n_z + 16):
            if row < n_x:
                k = kx_ref[brick * n_x + row].astype(jnp.float32)
            elif row < n_x + n_z:
                k = kz_ref[row - n_x].astype(jnp.float32)
            else:
                q = row - n_x - n_z
                k = float(q + 1 if q < 8 else 8 * (q - 7))
            kb_ref[row : row + 1, :] = jnp.full((1, LANES), k, jnp.float32)
        copies[3].wait()

    for frame in range(frames_here):
        counts = [counts_ref[frame, brick ^ d] for d in ids]
        starts = [jnp.int32(0)]
        for count in counts:
            starts.append(starts[-1] + (count + LANES - 1) // LANES)

        def build(item, slot, frame=frame, counts=counts, starts=starts):
            shard, start, count = jnp.int32(0), starts[0], counts[0]
            for s in range(1, n_shards):
                later = item >= starts[s]
                shard = jnp.where(later, s, shard)
                start = jnp.where(later, starts[s], start)
                count = jnp.where(later, counts[s], count)
            offset = (item - start) * LANES
            where = pl.ds(pl.multiple_of(jnp.minimum(offset, capacity - LANES), LANES), LANES)
            x = pos_ref[shard, 0, pl.ds(frame, 1), where]
            y = pos_ref[shard, 1, pl.ds(frame, 1), where]
            z = pos_ref[shard, 2, pl.ds(frame, 1), where]
            cx, sx = cis(kb_ref[0:n_x, :] * x)
            cz, sz = cis(kb_ref[n_x : n_x + n_z, :] * z)
            cy, sy = cis(kb_ref[n_x + n_z : n_x + n_z + 16, :] * y)
            live = lane + offset < count
            cz = jnp.where(live, cz, 0.0)
            sz = jnp.where(live, sz, 0.0)
            to = pl.ds(pl.multiple_of(item * LANES, LANES), LANES)
            half = n_x + 8
            base = slot * 2 * half
            row_ref[base : base + half, :] = jnp.concatenate([cx, cy[8:16]], axis=0)
            row_ref[base + half : base + 2 * half, :] = jnp.concatenate([sx, sy[8:16]], axis=0)

            def spread(q):
                return (
                    row_ref[pl.ds(base + q, 8, stride=0), :],
                    row_ref[pl.ds(base + half + q, 8, stride=0), :],
                )

            for i in range(0, n_x, 2):
                re, im = [], []
                for q in (i, i + 1):
                    a, b = spread(q)
                    re.append(a * cz - b * sz)
                    im.append(b * cz + a * sz)
                at = i * n_z
                left_ref[at : at + 2 * n_z, to] = jnp.concatenate(re, axis=0).astype(jnp.bfloat16)
                at += rows
                left_ref[at : at + 2 * n_z, to] = jnp.concatenate(im, axis=0).astype(jnp.bfloat16)
            ce, se = cy[0:8], sy[0:8]
            re, im = [ce], [se]
            for q in range(7):
                a, b = spread(n_x + q)
                re.append(a * ce - b * se)
                im.append(b * ce + a * se)
            for q in range(0, 8, 2):
                right_ref[8 * q : 8 * q + 16, to] = jnp.concatenate(re[q : q + 2], axis=0).astype(jnp.bfloat16)
                right_ref[KMAX + 8 * q : KMAX + 8 * q + 16, to] = jnp.concatenate(im[q : q + 2], axis=0).astype(jnp.bfloat16)

        def build_unit(unit, carry, build=build):
            for g in range(UNIT):
                build(unit * UNIT + g, g)
            return carry

        units = (starts[-1] + UNIT - 1) // UNIT
        lax.fori_loop(0, units, build_unit, 0)
        prod_ref = outs[0].at[frame] if not last else outs[-1].at[frame]
        prod_ref[...] = jnp.zeros(prod_ref.shape, jnp.float32) if first else prod_in[frame]

        def multiply(width):
            def step(base):
                where = pl.ds(pl.multiple_of(base, UNIT * LANES), width)
                prod_ref[...] += lax.dot_general(
                    left_ref[:, where],
                    right_ref[:, where],
                    (((1,), (1,)), ((), ())),
                    preferred_element_type=jnp.float32,
                )

            return step

        wide = multiply(BIG * UNIT * LANES)
        full = units // BIG

        def wide_step(i, carry, wide=wide):
            wide(i * (BIG * UNIT * LANES))
            return carry

        lax.fori_loop(0, full, wide_step, 0)
        for rest in range(1, BIG):

            @pl.when(units - full * BIG == rest)
            def _(rest=rest, multiply=multiply, full=full):
                multiply(rest * UNIT * LANES)(full * (BIG * UNIT * LANES))

    if last:
        copies[1].wait()
        send_own_rows(outs, groups, rows, share, frames_here, local[1])


def send_own_rows(outs, groups, rows, share, frames_here, ky_ref):
    prods = outs[-1]
    width = groups * share
    group = lax.axis_index("frames")
    column = lax.broadcasted_iota(jnp.int32, (1, width), 1)
    wanted = jnp.zeros((1, width), jnp.int32)
    for dest in range(groups):
        base = (group ^ dest) * share
        for j in range(share):
            wanted = jnp.where(column == dest * share + j, ky_ref[base + j], wanted)
    ks = lax.broadcasted_iota(jnp.int32, (KMAX, width), 0) + 1
    hot = jnp.where(ks == wanted, 1.0, 0.0).astype(jnp.bfloat16)
    none = jnp.zeros_like(hot)
    hot = jnp.concatenate(
        [jnp.concatenate([hot, none], axis=1), jnp.concatenate([none, hot], axis=1)], axis=0
    )
    hot = jnp.concatenate([hot, hot, hot], axis=0)
    first_half = lax.broadcasted_iota(jnp.int32, (rows, 2 * KMAX), 1) < KMAX
    for frame in range(frames_here):
        top = prods[frame, 0:rows, :]
        low = pltpu.roll(prods[frame, rows : 2 * rows, :], KMAX, 1)
        terms = jnp.where(first_half, top - low, -(top + low))
        hi = terms.astype(jnp.bfloat16)
        rest = terms - hi.astype(jnp.float32)
        mid = rest.astype(jnp.bfloat16)
        tail = (rest - mid.astype(jnp.float32)).astype(jnp.bfloat16)
        split = jnp.concatenate([hi, mid, tail], axis=1)
        picked = lax.dot_general(
            hot, split, (((0,), (1,)), ((), ())), preferred_element_type=jnp.float32
        )
        for part in range(2):
            for dest in range(groups):
                at = part * width + dest * share
                to = (frame * 2 + part) * share
                outs[dest][to : to + share, :] = picked[at : at + share, :]


def dft_table(table_ref, frames_total, atoms):
    weights = [0.5 - 0.5 * math.cos(2.0 * math.pi * (t + 0.5) / frames_total) for t in range(frames_total)]
    scale = 1.0 / math.sqrt(atoms * sum(w * w for w in weights))
    shape = (2 * frames_total, NW)
    row = lax.broadcasted_iota(jnp.int32, shape, 0)
    time = row // 2
    real = row % 2 == 0
    freq = lax.broadcasted_iota(jnp.int32, shape, 1)
    window = 0.5 - 0.5 * cis((time.astype(jnp.float32) + 0.5) / frames_total)[0]
    c, s = cis((time * freq % NW).astype(jnp.float32) / NW)
    cw, sw = scale * window * c, scale * window * s
    full = jnp.concatenate([jnp.where(real, cw, sw), jnp.where(real, -sw, cw)], axis=1)
    hi = full.astype(jnp.bfloat16)
    lo = (full - hi.astype(jnp.float32)).astype(jnp.bfloat16)
    none = jnp.zeros_like(hi)
    size = 2 * frames_total
    for split, part in enumerate((hi, lo, hi)):
        at = split * 2 * size
        table_ref[at : at + size, :] = jnp.concatenate([part, none], axis=1)
        table_ref[at + size : at + 2 * size, :] = jnp.concatenate([none, part], axis=1)


def spectrum_kernel(groups, share, chunk, n_x, n_z, frames_total, atoms, *refs):
    srcs = refs[:groups]
    out_ref, all_ref, table_ref = refs[groups:]
    block = srcs[0].shape[0]
    terms = groups * block // share

    @pl.when(pl.program_id(0) == 0)
    def _():
        for distance in range(groups):
            at = pl.multiple_of((lax.axis_index("frames") ^ distance) * block, block)
            all_ref[pl.ds(at, block), :] = srcs[distance][...]
        dft_table(table_ref, frames_total, atoms)

    base = pl.program_id(0) * chunk
    for pair in range(chunk // 2):
        j = base + 2 * pair
        x = jnp.concatenate(
            [all_ref[pl.ds(j + q, terms, stride=share), :] for q in range(2)], axis=0
        )
        hi = x.astype(jnp.bfloat16)
        lo = (x - hi.astype(jnp.float32)).astype(jnp.bfloat16)
        y = lax.dot_general(
            jnp.concatenate([hi, hi, lo], axis=0),
            table_ref[...],
            (((0,), (0,)), ((), ())),
            preferred_element_type=jnp.float32,
        )
        for q in range(2):
            re = y[:, 2 * q * NW : (2 * q + 1) * NW]
            im = y[:, (2 * q + 1) * NW : (2 * q + 2) * NW]
            out_ref[:, 2 * pair + q] = (re * re + im * im).reshape(n_x, n_z, NW)


def swap(value, axis, size, distance):
    return lax.ppermute(value, axis, [(i, i ^ distance) for i in range(size)])


def per_device(positions, counts, kvec_x, kvec_y, kvec_z):
    groups = lax.axis_size("frames")
    bricks = lax.axis_size("bricks")
    frames_here, capacity = positions.shape[1], positions.shape[2]
    n_x, n_z = kvec_x.shape[0] // bricks, kvec_z.shape[0]
    rows = n_x * n_z
    share = kvec_y.shape[0] // groups
    block = frames_here * 2 * share
    vmem = pl.BlockSpec(memory_space=pltpu.VMEM)
    prods_shape = (frames_here, 2 * rows, 2 * KMAX)
    waves_shape = (n_x + n_z + 16, LANES)
    hbm = pl.BlockSpec(memory_space=pltpu.HBM)

    def density(shards, ids, sums, last):
        first = sums is None
        lanes = -(-len(ids) * capacity // (BIG * UNIT * LANES)) * BIG * UNIT * LANES
        args = [counts]
        if first:
            args += [kvec_x, kvec_z, shards]
        elif last:
            args += [kvec_y]
        scratch = [pltpu.SMEM(arg.shape, jnp.int32) for arg in args[:3]]
        if first:
            scratch.append(pltpu.VMEM(shards.shape, jnp.float32))
        scratch += [
            pltpu.VMEM((2 * rows, lanes), jnp.bfloat16),
            pltpu.VMEM((2 * KMAX, lanes), jnp.bfloat16),
            pltpu.VMEM((UNIT * 2 * (n_x + 8), LANES), jnp.float32),
            pltpu.SemaphoreType.DMA((len(args),)),
        ]
        if last:
            out_shape = [jax.ShapeDtypeStruct((block, rows), jnp.float32)] * groups
            scratch = [pltpu.VMEM(prods_shape, jnp.float32)] + scratch
        else:
            out_shape = [jax.ShapeDtypeStruct(prods_shape, jnp.float32)]
            if first:
                out_shape.append(jax.ShapeDtypeStruct(waves_shape, jnp.float32))
        atoms = frames_here * len(ids) * capacity
        return pl.pallas_call(
            functools.partial(density_kernel, ids, first, last, groups, n_x, n_z, share),
            out_shape=out_shape,
            in_specs=[hbm] * len(args) + [vmem] * (0 if first else 3),
            out_specs=[vmem] * len(out_shape),
            scratch_shapes=scratch,
            cost_estimate=pl.CostEstimate(
                flops=atoms * rows * KMAX * 8, bytes_accessed=atoms * 12, transcendentals=0
            ),
            compiler_params=pltpu.CompilerParams(vmem_limit_bytes=48 << 20),
            name="density",
        )(*args, *([] if first else [shards, *sums]))

    held, fresh, ids = positions[None], positions[None], [0]
    new, sums, waves = [0], None, None
    distance = bricks // 2
    while distance:
        got = swap(held, "bricks", bricks, distance)
        out = density(fresh, new, sums, False)
        waves = out[1] if sums is None else waves
        got, prods = lax.optimization_barrier((got, out[0]))
        sums = (prods, waves)
        new = [i ^ distance for i in ids]
        ids, fresh = ids + new, got
        distance //= 2
        if distance:
            held = jnp.concatenate([held, got], axis=0)
    sends = density(fresh, new, sums, True)
    got = [sends[0]] + [swap(sends[d], "frames", groups, d) for d in range(1, groups)]

    chunk = min(8, share)
    frames_total = frames_here * groups
    return pl.pallas_call(
        functools.partial(
            spectrum_kernel, groups, share, chunk, n_x, n_z, frames_total, capacity * bricks
        ),
        out_shape=jax.ShapeDtypeStruct((n_x, share, n_z, NW), jnp.float32),
        grid=(share // chunk,),
        in_specs=[vmem] * groups,
        out_specs=pl.BlockSpec((n_x, chunk, n_z, NW), lambda c: (0, c, 0, 0)),
        scratch_shapes=[
            pltpu.VMEM((groups * block, rows), jnp.float32),
            pltpu.VMEM((12 * frames_total, 4 * NW), jnp.bfloat16),
        ],
        compiler_params=pltpu.CompilerParams(vmem_limit_bytes=16 << 20),
        name="spectrum",
    )(*got)


def solution(mesh):
    return jax.shard_map(
        per_device,
        mesh=mesh,
        in_specs=(P(None, "frames", "bricks"), P("frames", None), P(), P(), P()),
        out_specs=P("bricks", "frames", None, None),
        check_vma=False,
    )
```

```python
import functools
import math

import jax
import jax.numpy as jnp
import numpy as np
from jax import lax
from jax.experimental import pallas as pl
from jax.experimental.pallas import tpu as pltpu
from jax.sharding import PartitionSpec as P

NW = 128
KMAX = 64
LANES = 128
UNIT = 4
BIG = 8

def _fit(fun, degree):
    nodes = 0.125 * (1.0 + np.cos(np.pi * (np.arange(64) + 0.5) / 64))
    series = np.polynomial.chebyshev.Chebyshev.fit(nodes, fun(np.sqrt(nodes)), degree, domain=[0.0, 0.25])
    return [float(c) for c in series.convert(kind=np.polynomial.Polynomial).coef]


COS_C = _fit(lambda f: math.sqrt(2.0) * np.cos(np.pi * f), 4)
SIN_C = _fit(lambda f: math.sqrt(2.0) * np.sin(np.pi * f) / f, 4)


def _poly(coefs, u):
    acc = coefs[-1] * u + coefs[-2]
    for c in coefs[-3::-1]:
        acc = acc * u + c
    return acc


def cis(turns):
    f = turns - jnp.round(turns)
    u = f * f
    half_c = _poly(COS_C, u)
    half_s = _poly(SIN_C, u) * f
    return 1.0 - half_s * half_s, half_s * half_c


def density_kernel(ids, first, last, groups, n_x, n_z, share, *refs):
    n_args = 4 if first else 1 if last else 0
    args, refs = refs[:n_args], refs[n_args:]
    left_ref, right_ref, row_ref, arg_sem = refs[-4:]
    refs = refs[:-4]
    if not first:
        (pos_ref, prod_in, kb_ref, counts_ref), refs = refs[:4], refs[4:]
    outs, local = refs[: len(refs) - n_args], refs[len(refs) - n_args :]
    copies = [
        pltpu.make_async_copy(args[i], local[i], arg_sem.at[i]) for i in range(n_args)
    ]
    for copy in copies:
        copy.start()
    if first:
        counts_ref, pos_ref, kb_ref = local[0], local[3], outs[1]
    rows = n_x * n_z
    n_shards, _, frames_here, capacity = pos_ref.shape
    brick = lax.axis_index("bricks")
    lane = lax.broadcasted_iota(jnp.int32, (n_z, LANES), 1)

    if first:
        kx_ref, kz_ref = local[1:3]
        copies[0].wait()
        for frame in range(frames_here):
            for at in range(counts_ref.shape[1]):
                outs[2][frame, at] = counts_ref[frame, at]
        copies[1].wait()
        copies[2].wait()
        for row in range(n_x + n_z + 16):
            if row < n_x:
                k = kx_ref[brick * n_x + row].astype(jnp.float32)
            elif row < n_x + n_z:
                k = kz_ref[row - n_x].astype(jnp.float32)
            else:
                q = row - n_x - n_z
                k = float(q + 1 if q < 8 else 8 * (q - 7))
            kb_ref[row : row + 1, :] = jnp.full((1, LANES), k, jnp.float32)
        copies[3].wait()

    for frame in range(frames_here):
        counts = [counts_ref[frame, brick ^ d] for d in ids]
        starts = [jnp.int32(0)]
        for count in counts:
            starts.append(starts[-1] + (count + LANES - 1) // LANES)

        def build(item, slot, frame=frame, counts=counts, starts=starts):
            shard, start, count = jnp.int32(0), starts[0], counts[0]
            for s in range(1, n_shards):
                later = item >= starts[s]
                shard = jnp.where(later, s, shard)
                start = jnp.where(later, starts[s], start)
                count = jnp.where(later, counts[s], count)
            offset = (item - start) * LANES
            where = pl.ds(pl.multiple_of(jnp.minimum(offset, capacity - LANES), LANES), LANES)
            x = pos_ref[shard, 0, pl.ds(frame, 1), where]
            y = pos_ref[shard, 1, pl.ds(frame, 1), where]
            z = pos_ref[shard, 2, pl.ds(frame, 1), where]
            cx, sx = cis(kb_ref[0:n_x, :] * x)
            cz, sz = cis(kb_ref[n_x : n_x + n_z, :] * z)
            cy, sy = cis(kb_ref[n_x + n_z : n_x + n_z + 16, :] * y)
            live = lane + offset < count
            cz = jnp.where(live, cz, 0.0)
            sz = jnp.where(live, sz, 0.0)
            to = pl.ds(pl.multiple_of(item * LANES, LANES), LANES)
            half = n_x + 8
            base = slot * 2 * half
            row_ref[base : base + half, :] = jnp.concatenate([cx, cy[8:16]], axis=0)
            row_ref[base + half : base + 2 * half, :] = jnp.concatenate([sx, sy[8:16]], axis=0)

            def spread(q):
                return (
                    row_ref[pl.ds(base + q, 8, stride=0), :],
                    row_ref[pl.ds(base + half + q, 8, stride=0), :],
                )

            for i in range(0, n_x, 2):
                re, im = [], []
                for q in (i, i + 1):
                    a, b = spread(q)
                    re.append(a * cz - b * sz)
                    im.append(b * cz + a * sz)
                at = i * n_z
                left_ref[at : at + 2 * n_z, to] = jnp.concatenate(re, axis=0).astype(jnp.bfloat16)
                at += rows
                left_ref[at : at + 2 * n_z, to] = jnp.concatenate(im, axis=0).astype(jnp.bfloat16)
            ce, se = cy[0:8], sy[0:8]
            re, im = [ce], [se]
            for q in range(7):
                a, b = spread(n_x + q)
                re.append(a * ce - b * se)
                im.append(b * ce + a * se)
            for q in range(0, 8, 2):
                right_ref[8 * q : 8 * q + 16, to] = jnp.concatenate(re[q : q + 2], axis=0).astype(jnp.bfloat16)
                right_ref[KMAX + 8 * q : KMAX + 8 * q + 16, to] = jnp.concatenate(im[q : q + 2], axis=0).astype(jnp.bfloat16)

        def build_unit(unit, carry, build=build):
            for g in range(UNIT):
                build(unit * UNIT + g, g)
            return carry

        units = (starts[-1] + UNIT - 1) // UNIT
        lax.fori_loop(0, units, build_unit, 0)
        prod_ref = outs[0].at[frame] if not last else outs[-1].at[frame]
        prod_ref[...] = jnp.zeros(prod_ref.shape, jnp.float32) if first else prod_in[frame]

        def multiply(width):
            def step(base):
                where = pl.ds(pl.multiple_of(base, UNIT * LANES), width)
                prod_ref[...] += lax.dot_general(
                    left_ref[:, where],
                    right_ref[:, where],
                    (((1,), (1,)), ((), ())),
                    preferred_element_type=jnp.float32,
                )

            return step

        wide = multiply(BIG * UNIT * LANES)
        full = units // BIG

        def wide_step(i, carry, wide=wide):
            wide(i * (BIG * UNIT * LANES))
            return carry

        lax.fori_loop(0, full, wide_step, 0)
        for rest in range(1, BIG):

            @pl.when(units - full * BIG == rest)
            def _(rest=rest, multiply=multiply, full=full):
                multiply(rest * UNIT * LANES)(full * (BIG * UNIT * LANES))

    if last:
        copies[0].wait()
        send_own_rows(outs, groups, rows, share, frames_here, local[0])


def send_own_rows(outs, groups, rows, share, frames_here, ky_ref):
    prods = outs[-1]
    width = groups * share
    group = lax.axis_index("frames")
    column = lax.broadcasted_iota(jnp.int32, (1, width), 1)
    parts = [
        jnp.where(column == dest * share + j, ky_ref[(group ^ dest) * share + j], 0)
        for dest in range(groups)
        for j in range(share)
    ]
    while len(parts) > 1:
        parts = [sum(parts[i : i + 2][1:], parts[i]) for i in range(0, len(parts), 2)]
    wanted = parts[0]
    ks = lax.broadcasted_iota(jnp.int32, (KMAX, width), 0) + 1
    hot = jnp.where(ks == wanted, 1.0, 0.0).astype(jnp.bfloat16)
    none = jnp.zeros_like(hot)
    hot = jnp.concatenate(
        [jnp.concatenate([hot, none], axis=1), jnp.concatenate([none, hot], axis=1)], axis=0
    )
    hot = jnp.concatenate([hot, hot, hot], axis=0)
    first_half = lax.broadcasted_iota(jnp.int32, (rows, 2 * KMAX), 1) < KMAX
    for frame in range(frames_here):
        top = prods[frame, 0:rows, :]
        low = pltpu.roll(prods[frame, rows : 2 * rows, :], KMAX, 1)
        terms = jnp.where(first_half, top - low, -(top + low))
        hi = terms.astype(jnp.bfloat16)
        rest = terms - hi.astype(jnp.float32)
        mid = rest.astype(jnp.bfloat16)
        tail = (rest - mid.astype(jnp.float32)).astype(jnp.bfloat16)
        split = jnp.concatenate([hi, mid, tail], axis=1)
        picked = lax.dot_general(
            hot, split, (((0,), (1,)), ((), ())), preferred_element_type=jnp.float32
        )
        for part in range(2):
            for dest in range(groups):
                at = part * width + dest * share
                to = (frame * 2 + part) * share
                outs[dest][to : to + share, :] = picked[at : at + share, :]


def dft_table(table_ref, frames_total, atoms):
    weights = [0.5 - 0.5 * math.cos(2.0 * math.pi * (t + 0.5) / frames_total) for t in range(frames_total)]
    scale = 1.0 / math.sqrt(atoms * sum(w * w for w in weights))
    shape = (2 * frames_total, NW)
    row = lax.broadcasted_iota(jnp.int32, shape, 0)
    time = row // 2
    real = row % 2 == 0
    freq = lax.broadcasted_iota(jnp.int32, shape, 1)
    window = 0.5 - 0.5 * cis((time.astype(jnp.float32) + 0.5) / frames_total)[0]
    c, s = cis((time * freq % NW).astype(jnp.float32) / NW)
    cw, sw = scale * window * c, scale * window * s
    full = jnp.concatenate([jnp.where(real, cw, sw), jnp.where(real, -sw, cw)], axis=1)
    hi = full.astype(jnp.bfloat16)
    lo = (full - hi.astype(jnp.float32)).astype(jnp.bfloat16)
    none = jnp.zeros_like(hi)
    size = 2 * frames_total
    for split, part in enumerate((hi, lo, hi)):
        at = split * 2 * size
        table_ref[at : at + size, :] = jnp.concatenate([part, none], axis=1)
        table_ref[at + size : at + 2 * size, :] = jnp.concatenate([none, part], axis=1)


def spectrum_kernel(groups, share, chunk, n_x, n_z, frames_total, atoms, *refs):
    srcs = refs[:groups]
    out_ref, all_ref, table_ref = refs[groups:]
    block = srcs[0].shape[0]
    terms = groups * block // share

    @pl.when(pl.program_id(0) == 0)
    def _():
        for distance in range(groups):
            at = pl.multiple_of((lax.axis_index("frames") ^ distance) * block, block)
            all_ref[pl.ds(at, block), :] = srcs[distance][...]
        dft_table(table_ref, frames_total, atoms)

    base = pl.program_id(0) * chunk
    for pair in range(chunk // 2):
        j = base + 2 * pair
        x = jnp.concatenate(
            [all_ref[pl.ds(j + q, terms, stride=share), :] for q in range(2)], axis=0
        )
        hi = x.astype(jnp.bfloat16)
        lo = (x - hi.astype(jnp.float32)).astype(jnp.bfloat16)
        y = lax.dot_general(
            jnp.concatenate([hi, hi, lo], axis=0),
            table_ref[...],
            (((0,), (0,)), ((), ())),
            preferred_element_type=jnp.float32,
        )
        for q in range(2):
            re = y[:, 2 * q * NW : (2 * q + 1) * NW]
            im = y[:, (2 * q + 1) * NW : (2 * q + 2) * NW]
            out_ref[:, 2 * pair + q] = (re * re + im * im).reshape(n_x, n_z, NW)


def swap(value, axis, size, distance):
    return lax.ppermute(value, axis, [(i, i ^ distance) for i in range(size)])


def per_device(positions, counts, kvec_x, kvec_y, kvec_z):
    groups = lax.axis_size("frames")
    bricks = lax.axis_size("bricks")
    frames_here, capacity = positions.shape[1], positions.shape[2]
    n_x, n_z = kvec_x.shape[0] // bricks, kvec_z.shape[0]
    rows = n_x * n_z
    share = kvec_y.shape[0] // groups
    block = frames_here * 2 * share
    vmem = pl.BlockSpec(memory_space=pltpu.VMEM)
    prods_shape = (frames_here, 2 * rows, 2 * KMAX)
    waves_shape = (n_x + n_z + 16, LANES)
    hbm = pl.BlockSpec(memory_space=pltpu.HBM)
    smem = pl.BlockSpec(memory_space=pltpu.SMEM)

    def density(shards, ids, sums, last):
        first = sums is None
        lanes = -(-len(ids) * capacity // (BIG * UNIT * LANES)) * BIG * UNIT * LANES
        args = [counts, kvec_x, kvec_z, shards] if first else [kvec_y] if last else []
        args = [pltpu.with_memory_space_constraint(arg, pltpu.HBM) for arg in args]
        scratch = [pltpu.SMEM(arg.shape, jnp.int32) for arg in args[:3]]
        if first:
            scratch.append(pltpu.VMEM(shards.shape, jnp.float32))
        scratch += [
            pltpu.VMEM((2 * rows, lanes), jnp.bfloat16),
            pltpu.VMEM((2 * KMAX, lanes), jnp.bfloat16),
            pltpu.VMEM((UNIT * 2 * (n_x + 8), LANES), jnp.float32),
            pltpu.SemaphoreType.DMA((4,)),
        ]
        if last:
            out_shape = [jax.ShapeDtypeStruct((block, rows), jnp.float32)] * groups
            scratch = [pltpu.VMEM(prods_shape, jnp.float32)] + scratch
        else:
            out_shape = [jax.ShapeDtypeStruct(prods_shape, jnp.float32)]
            if first:
                out_shape.append(jax.ShapeDtypeStruct(waves_shape, jnp.float32))
                out_shape.append(jax.ShapeDtypeStruct(counts.shape, jnp.int32))
        atoms = frames_here * len(ids) * capacity
        return pl.pallas_call(
            functools.partial(density_kernel, ids, first, last, groups, n_x, n_z, share),
            out_shape=out_shape,
            in_specs=[hbm] * len(args) + ([] if first else [vmem] * 3 + [smem]),
            out_specs=[vmem, vmem, smem] if first else [vmem] * len(out_shape),
            scratch_shapes=scratch,
            cost_estimate=pl.CostEstimate(
                flops=atoms * rows * KMAX * 8, bytes_accessed=atoms * 12, transcendentals=0
            ),
            compiler_params=pltpu.CompilerParams(vmem_limit_bytes=48 << 20),
            name="density",
        )(*args, *([] if first else [shards, *sums]))

    held, fresh, ids = positions[None], positions[None], [0]
    new, sums, fixed = [0], None, None
    distance = bricks // 2
    while distance:
        got = swap(held, "bricks", bricks, distance)
        out = density(fresh, new, sums, False)
        fixed = out[1:] if sums is None else fixed
        got, prods = lax.optimization_barrier((got, out[0]))
        sums = (prods, *fixed)
        new = [i ^ distance for i in ids]
        ids, fresh = ids + new, got
        distance //= 2
        if distance:
            held = jnp.concatenate([held, got], axis=0)
    sends = density(fresh, new, sums, True)
    got = [sends[0]] + [swap(sends[d], "frames", groups, d) for d in range(1, groups)]

    chunk = min(8, share)
    frames_total = frames_here * groups
    return pl.pallas_call(
        functools.partial(
            spectrum_kernel, groups, share, chunk, n_x, n_z, frames_total, capacity * bricks
        ),
        out_shape=jax.ShapeDtypeStruct((n_x, share, n_z, NW), jnp.float32),
        grid=(share // chunk,),
        in_specs=[vmem] * groups,
        out_specs=pl.BlockSpec((n_x, chunk, n_z, NW), lambda c: (0, c, 0, 0)),
        scratch_shapes=[
            pltpu.VMEM((groups * block, rows), jnp.float32),
            pltpu.VMEM((12 * frames_total, 4 * NW), jnp.bfloat16),
        ],
        compiler_params=pltpu.CompilerParams(vmem_limit_bytes=16 << 20),
        name="spectrum",
    )(*got)


def solution(mesh):
    return jax.shard_map(
        per_device,
        mesh=mesh,
        in_specs=(P(None, "frames", "bricks"), P("frames", None), P(), P(), P()),
        out_specs=P("bricks", "frames", None, None),
        check_vma=False,
    )
```

```python
import functools
import math

import jax
import jax.numpy as jnp
import numpy as np
from jax import lax
from jax.experimental import pallas as pl
from jax.experimental.pallas import tpu as pltpu
from jax.sharding import PartitionSpec as P

NW = 128
KMAX = 64
LANES = 128
UNIT = 4
PAIRS = 2
BIG = 8

def _fit(fun, degree):
    nodes = 0.125 * (1.0 + np.cos(np.pi * (np.arange(64) + 0.5) / 64))
    series = np.polynomial.chebyshev.Chebyshev.fit(nodes, fun(np.sqrt(nodes)), degree, domain=[0.0, 0.25])
    return [float(c) for c in series.convert(kind=np.polynomial.Polynomial).coef]


COS_C = _fit(lambda f: math.sqrt(2.0) * np.cos(np.pi * f), 4)
SIN_C = _fit(lambda f: math.sqrt(2.0) * np.sin(np.pi * f) / f, 4)


def _poly(coefs, u):
    acc = coefs[-1] * u + coefs[-2]
    for c in coefs[-3::-1]:
        acc = acc * u + c
    return acc


def cis(turns):
    f = turns - jnp.round(turns)
    u = f * f
    half_c = _poly(COS_C, u)
    half_s = _poly(SIN_C, u) * f
    return 1.0 - half_s * half_s, half_s * half_c


def density_kernel(ids, first, last, groups, n_x, n_z, share, *refs):
    n_args = 4 if first else 1 if last else 0
    args, refs = refs[:n_args], refs[n_args:]
    left_ref, right_ref, row_ref, arg_sem = refs[-4:]
    refs = refs[:-4]
    if not first:
        (pos_ref, prod_in, kb_ref, counts_ref), refs = refs[:4], refs[4:]
    n_local = min(n_args, 3)
    outs, local = refs[: len(refs) - n_local], refs[len(refs) - n_local :]
    if first:
        local = (*local, outs[3])
    copies = [
        pltpu.make_async_copy(args[i], local[i], arg_sem.at[i]) for i in range(n_args)
    ]
    for copy in copies:
        copy.start()
    if first:
        counts_ref, pos_ref, kb_ref = local[0], local[3], outs[1]
    rows = n_x * n_z
    n_shards, _, frames_here, capacity = pos_ref.shape
    brick = lax.axis_index("bricks")
    lane = lax.broadcasted_iota(jnp.int32, (n_z, LANES), 1)

    if first:
        kx_ref, kz_ref = local[1:3]
        copies[0].wait()
        for frame in range(frames_here):
            for at in range(counts_ref.shape[1]):
                outs[2][frame, at] = counts_ref[frame, at]
        copies[1].wait()
        copies[2].wait()
        for row in range(n_x + n_z + 16):
            if row < n_x:
                k = kx_ref[brick * n_x + row].astype(jnp.float32)
            elif row < n_x + n_z:
                k = kz_ref[row - n_x].astype(jnp.float32)
            else:
                q = row - n_x - n_z
                k = float(q + 1 if q < 8 else 8 * (q - 7))
            kb_ref[row : row + 1, :] = jnp.full((1, LANES), k, jnp.float32)
        copies[3].wait()

    for frame in range(frames_here):
        counts = [counts_ref[frame, brick ^ d] for d in ids]
        starts = [jnp.int32(0)]
        for count in counts:
            starts.append(starts[-1] + (count + LANES - 1) // LANES)

        def build(item, slot, frame=frame, counts=counts, starts=starts):
            shard, start, count = jnp.int32(0), starts[0], counts[0]
            for s in range(1, n_shards):
                later = item >= starts[s]
                shard = jnp.where(later, s, shard)
                start = jnp.where(later, starts[s], start)
                count = jnp.where(later, counts[s], count)
            offset = (item - start) * LANES
            where = pl.ds(pl.multiple_of(jnp.minimum(offset, capacity - LANES), LANES), LANES)
            x = pos_ref[shard, 0, pl.ds(frame, 1), where]
            y = pos_ref[shard, 1, pl.ds(frame, 1), where]
            z = pos_ref[shard, 2, pl.ds(frame, 1), where]
            cx, sx = cis(kb_ref[0:n_x, :] * x)
            cz, sz = cis(kb_ref[n_x : n_x + n_z, :] * z)
            cy, sy = cis(kb_ref[n_x + n_z : n_x + n_z + 16, :] * y)
            live = lane + offset < count
            cz = jnp.where(live, cz, 0.0)
            sz = jnp.where(live, sz, 0.0)
            to = pl.ds(pl.multiple_of(item * LANES, LANES), LANES)
            half = n_x + 8
            base = slot * 2 * half
            row_ref[base : base + half, :] = jnp.concatenate([cx, cy[8:16]], axis=0)
            row_ref[base + half : base + 2 * half, :] = jnp.concatenate([sx, sy[8:16]], axis=0)

            def spread(q):
                return (
                    row_ref[pl.ds(base + q, 8, stride=0), :],
                    row_ref[pl.ds(base + half + q, 8, stride=0), :],
                )

            for i in range(0, n_x, 2):
                re, im = [], []
                for q in (i, i + 1):
                    a, b = spread(q)
                    re.append(a * cz - b * sz)
                    im.append(b * cz + a * sz)
                at = i * n_z
                left_ref[at : at + 2 * n_z, to] = jnp.concatenate(re, axis=0).astype(jnp.bfloat16)
                at += rows
                left_ref[at : at + 2 * n_z, to] = jnp.concatenate(im, axis=0).astype(jnp.bfloat16)
            ce, se = cy[0:8], sy[0:8]
            re, im = [ce], [se]
            for q in range(7):
                a, b = spread(n_x + q)
                re.append(a * ce - b * se)
                im.append(b * ce + a * se)
            for q in range(0, 8, 2):
                right_ref[8 * q : 8 * q + 16, to] = jnp.concatenate(re[q : q + 2], axis=0).astype(jnp.bfloat16)
                right_ref[KMAX + 8 * q : KMAX + 8 * q + 16, to] = jnp.concatenate(im[q : q + 2], axis=0).astype(jnp.bfloat16)

        def build_unit(unit, carry, build=build):
            for g in range(UNIT):
                build(unit * UNIT + g, g)
            return carry

        units = (starts[-1] + UNIT - 1) // UNIT
        lax.fori_loop(0, units, build_unit, 0)
        prod_ref = outs[0].at[frame] if not last else outs[-1].at[frame]
        prod_ref[...] = jnp.zeros(prod_ref.shape, jnp.float32) if first else prod_in[frame]

        def multiply(width):
            def step(base):
                where = pl.ds(pl.multiple_of(base, UNIT * LANES), width)
                prod_ref[...] += lax.dot_general(
                    left_ref[:, where],
                    right_ref[:, where],
                    (((1,), (1,)), ((), ())),
                    preferred_element_type=jnp.float32,
                )

            return step

        wide = multiply(BIG * UNIT * LANES)
        full = units // BIG

        def wide_step(i, carry, wide=wide):
            wide(i * (BIG * UNIT * LANES))
            return carry

        lax.fori_loop(0, full, wide_step, 0)
        for rest in range(1, BIG):

            @pl.when(units - full * BIG == rest)
            def _(rest=rest, multiply=multiply, full=full):
                multiply(rest * UNIT * LANES)(full * (BIG * UNIT * LANES))

    if last:
        copies[0].wait()
        send_own_rows(outs, groups, rows, share, frames_here, local[0])


def send_own_rows(outs, groups, rows, share, frames_here, ky_ref):
    prods = outs[-1]
    width = groups * share
    group = lax.axis_index("frames")
    column = lax.broadcasted_iota(jnp.int32, (1, width), 1)
    parts = [
        jnp.where(column == dest * share + j, ky_ref[(group ^ dest) * share + j], 0)
        for dest in range(groups)
        for j in range(share)
    ]
    while len(parts) > 1:
        parts = [sum(parts[i : i + 2][1:], parts[i]) for i in range(0, len(parts), 2)]
    wanted = parts[0]
    ks = lax.broadcasted_iota(jnp.int32, (KMAX, width), 0) + 1
    hot = jnp.where(ks == wanted, 1.0, 0.0).astype(jnp.bfloat16)
    none = jnp.zeros_like(hot)
    hot = jnp.concatenate(
        [jnp.concatenate([hot, none], axis=1), jnp.concatenate([none, hot], axis=1)], axis=0
    )
    hot = jnp.concatenate([hot, hot, hot], axis=0)
    first_half = lax.broadcasted_iota(jnp.int32, (rows, 2 * KMAX), 1) < KMAX
    for frame in range(frames_here):
        top = prods[frame, 0:rows, :]
        low = pltpu.roll(prods[frame, rows : 2 * rows, :], KMAX, 1)
        terms = jnp.where(first_half, top - low, -(top + low))
        hi = terms.astype(jnp.bfloat16)
        rest = terms - hi.astype(jnp.float32)
        mid = rest.astype(jnp.bfloat16)
        tail = (rest - mid.astype(jnp.float32)).astype(jnp.bfloat16)
        split = jnp.concatenate([hi, mid, tail], axis=1)
        picked = lax.dot_general(
            hot, split, (((0,), (1,)), ((), ())), preferred_element_type=jnp.float32
        )
        for part in range(2):
            for dest in range(groups):
                at = part * width + dest * share
                to = (frame * 2 + part) * share
                outs[dest][to : to + share, :] = picked[at : at + share, :]


def dft_table(table_ref, frames_total, atoms):
    weights = [0.5 - 0.5 * math.cos(2.0 * math.pi * (t + 0.5) / frames_total) for t in range(frames_total)]
    scale = 1.0 / math.sqrt(atoms * sum(w * w for w in weights))
    shape = (2 * frames_total, NW)
    row = lax.broadcasted_iota(jnp.int32, shape, 0)
    time = row // 2
    real = row % 2 == 0
    freq = lax.broadcasted_iota(jnp.int32, shape, 1)
    window = 0.5 - 0.5 * cis((time.astype(jnp.float32) + 0.5) / frames_total)[0]
    c, s = cis((time * freq % NW).astype(jnp.float32) / NW)
    cw, sw = scale * window * c, scale * window * s
    full = jnp.concatenate([jnp.where(real, cw, sw), jnp.where(real, -sw, cw)], axis=1)
    hi = full.astype(jnp.bfloat16)
    lo = (full - hi.astype(jnp.float32)).astype(jnp.bfloat16)
    none = jnp.zeros_like(hi)
    size = 2 * frames_total
    for split, part in enumerate((hi, lo, hi)):
        at = split * 2 * size
        table_ref[at : at + size, :] = jnp.concatenate([part, none], axis=1)
        table_ref[at + size : at + 2 * size, :] = jnp.concatenate([none, part], axis=1)


def spectrum_kernel(groups, share, chunk, n_x, n_z, frames_total, atoms, *refs):
    srcs = refs[:groups]
    out_hbm, out_ref, all_ref, table_ref, sem = refs[groups:]
    block = srcs[0].shape[0]
    terms = groups * block // share
    rows = n_x * n_z
    for distance in range(groups):
        at = pl.multiple_of((lax.axis_index("frames") ^ distance) * block, block)
        all_ref[pl.ds(at, block), :] = srcs[distance][...]
    dft_table(table_ref, frames_total, atoms)

    copies = []
    for base in range(0, share, chunk):
        for first in range(base, base + chunk, 2 * PAIRS):
            stacks = []
            for j in range(first, first + 2 * PAIRS, 2):
                x = jnp.concatenate(
                    [all_ref[pl.ds(j + q, terms, stride=share), :] for q in range(2)], axis=0
                )
                hi = x.astype(jnp.bfloat16)
                lo = (x - hi.astype(jnp.float32)).astype(jnp.bfloat16)
                stacks.append(jnp.concatenate([hi, hi, lo], axis=0))
            y = lax.dot_general(
                jnp.concatenate(stacks, axis=1),
                table_ref[...],
                (((0,), (0,)), ((), ())),
                preferred_element_type=jnp.float32,
            )
            for q in range(2 * PAIRS):
                own = y[q // 2 * rows : (q // 2 + 1) * rows]
                at = q % 2 * 2 * NW
                re, im = own[:, at : at + NW], own[:, at + NW : at + 2 * NW]
                out_ref[:, first + q] = (re * re + im * im).reshape(n_x, n_z, NW)
        part = pl.ds(base, chunk)
        copies.append(
            pltpu.make_async_copy(
                out_ref.at[:, part], out_hbm.at[:, part], sem.at[base // chunk]
            )
        )
        copies[-1].start()
    for copy in copies:
        copy.wait()


def swap(value, axis, size, distance):
    return lax.ppermute(value, axis, [(i, i ^ distance) for i in range(size)])


def per_device(positions, counts, kvec_x, kvec_y, kvec_z):
    groups = lax.axis_size("frames")
    bricks = lax.axis_size("bricks")
    frames_here, capacity = positions.shape[1], positions.shape[2]
    n_x, n_z = kvec_x.shape[0] // bricks, kvec_z.shape[0]
    rows = n_x * n_z
    share = kvec_y.shape[0] // groups
    block = frames_here * 2 * share
    vmem = pl.BlockSpec(memory_space=pltpu.VMEM)
    prods_shape = (frames_here, 2 * rows, 2 * KMAX)
    waves_shape = (n_x + n_z + 16, LANES)
    hbm = pl.BlockSpec(memory_space=pltpu.HBM)
    smem = pl.BlockSpec(memory_space=pltpu.SMEM)

    def density(shards, ids, sums, last):
        first = sums is None
        lanes = -(-len(ids) * capacity // (BIG * UNIT * LANES)) * BIG * UNIT * LANES
        args = [counts, kvec_x, kvec_z, shards] if first else [kvec_y] if last else []
        args = [pltpu.with_memory_space_constraint(arg, pltpu.HBM) for arg in args]
        scratch = [pltpu.SMEM(arg.shape, jnp.int32) for arg in args[:3]]
        scratch += [
            pltpu.VMEM((2 * rows, lanes), jnp.bfloat16),
            pltpu.VMEM((2 * KMAX, lanes), jnp.bfloat16),
            pltpu.VMEM((UNIT * 2 * (n_x + 8), LANES), jnp.float32),
            pltpu.SemaphoreType.DMA((4,)),
        ]
        if last:
            out_shape = [jax.ShapeDtypeStruct((block, rows), jnp.float32)] * groups
            scratch = [pltpu.VMEM(prods_shape, jnp.float32)] + scratch
        else:
            out_shape = [jax.ShapeDtypeStruct(prods_shape, jnp.float32)]
            if first:
                out_shape.append(jax.ShapeDtypeStruct(waves_shape, jnp.float32))
                out_shape.append(jax.ShapeDtypeStruct(counts.shape, jnp.int32))
                out_shape.append(jax.ShapeDtypeStruct(shards.shape, jnp.float32))
        atoms = frames_here * len(ids) * capacity
        return pl.pallas_call(
            functools.partial(density_kernel, ids, first, last, groups, n_x, n_z, share),
            out_shape=out_shape,
            in_specs=[hbm] * len(args) + ([] if first else [vmem] * 3 + [smem]),
            out_specs=[vmem, vmem, smem, vmem] if first else [vmem] * len(out_shape),
            scratch_shapes=scratch,
            cost_estimate=pl.CostEstimate(
                flops=atoms * rows * KMAX * 8, bytes_accessed=atoms * 12, transcendentals=0
            ),
            compiler_params=pltpu.CompilerParams(vmem_limit_bytes=48 << 20),
            name="density",
        )(*args, *([] if first else [shards, *sums]))

    held, fresh, ids = positions[None], positions[None], [0]
    new, sums, fixed = [0], None, None
    distance = bricks // 2
    while distance:
        got = swap(held, "bricks", bricks, distance)
        out = density(fresh, new, sums, False)
        if sums is None:
            fixed, held = out[1:3], out[3]
        got, prods = lax.optimization_barrier((got, out[0]))
        sums = (prods, *fixed)
        new = [i ^ distance for i in ids]
        ids, fresh = ids + new, got
        distance //= 2
        if distance:
            held = jnp.concatenate([held, got], axis=0)
    sends = density(fresh, new, sums, True)
    got = [sends[0]] + [swap(sends[d], "frames", groups, d) for d in range(1, groups)]

    chunk = min(8, share)
    frames_total = frames_here * groups
    return pl.pallas_call(
        functools.partial(
            spectrum_kernel, groups, share, chunk, n_x, n_z, frames_total, capacity * bricks
        ),
        out_shape=jax.ShapeDtypeStruct((n_x, share, n_z, NW), jnp.float32),
        in_specs=[vmem] * groups,
        out_specs=hbm,
        scratch_shapes=[
            pltpu.VMEM((n_x, share, n_z, NW), jnp.float32),
            pltpu.VMEM((groups * block, rows), jnp.float32),
            pltpu.VMEM((12 * frames_total, 4 * NW), jnp.bfloat16),
            pltpu.SemaphoreType.DMA((share // chunk,)),
        ],
        compiler_params=pltpu.CompilerParams(vmem_limit_bytes=16 << 20),
        name="spectrum",
    )(*got)


def solution(mesh):
    return jax.shard_map(
        per_device,
        mesh=mesh,
        in_specs=(P(None, "frames", "bricks"), P("frames", None), P(), P(), P()),
        out_specs=P("bricks", "frames", None, None),
        check_vma=False,
    )
```

```python
import functools
import math

import jax
import jax.numpy as jnp
import numpy as np
from jax import lax
from jax.experimental import pallas as pl
from jax.experimental.pallas import tpu as pltpu
from jax.sharding import PartitionSpec as P

NW = 128
KMAX = 64
LANES = 128
UNIT = 4
PAIRS = 2
BIG = 8

def _fit(fun, degree):
    nodes = 0.125 * (1.0 + np.cos(np.pi * (np.arange(64) + 0.5) / 64))
    series = np.polynomial.chebyshev.Chebyshev.fit(nodes, fun(np.sqrt(nodes)), degree, domain=[0.0, 0.25])
    return [float(c) for c in series.convert(kind=np.polynomial.Polynomial).coef]


COS_C = _fit(lambda f: math.sqrt(2.0) * np.cos(np.pi * f), 4)
SIN_C = _fit(lambda f: math.sqrt(2.0) * np.sin(np.pi * f) / f, 4)


def _poly(coefs, u):
    acc = coefs[-1] * u + coefs[-2]
    for c in coefs[-3::-1]:
        acc = acc * u + c
    return acc


def cis(turns):
    f = turns - jnp.round(turns)
    u = f * f
    half_c = _poly(COS_C, u)
    half_s = _poly(SIN_C, u) * f
    return 1.0 - half_s * half_s, half_s * half_c


def density_kernel(unit, low, ids, first, last, groups, n_x, n_z, share, *refs):
    n_args = 3 if first else 1 if last else 0
    args, refs = refs[:n_args], refs[n_args:]
    left_ref, right_ref, row_ref, arg_sem = refs[-4:]
    refs = refs[:-4]
    pos_ref, refs = refs[0], refs[1:]
    if not first:
        (prod_in, kb_ref, counts_ref), refs = refs[:3], refs[3:]
    outs, local = refs[: len(refs) - n_args], refs[len(refs) - n_args :]
    copies = [
        pltpu.make_async_copy(args[i], local[i], arg_sem.at[i]) for i in range(n_args)
    ]
    for copy in copies:
        copy.start()
    if first:
        counts_ref, kb_ref = local[0], outs[1]
    rows = n_x * n_z
    _, _, frames_here, capacity = pos_ref.shape
    n_shards = len(ids)
    brick = lax.axis_index("bricks")
    lane = lax.broadcasted_iota(jnp.int32, (n_z, LANES), 1)

    if first:
        kx_ref, kz_ref = local[1:3]
        copies[0].wait()
        for frame in range(frames_here):
            for at in range(counts_ref.shape[1]):
                outs[2][frame, at] = counts_ref[frame, at]
        copies[1].wait()
        copies[2].wait()
        for row in range(n_x + n_z + 16):
            if row < n_x:
                k = kx_ref[brick * n_x + row].astype(jnp.float32)
            elif row < n_x + n_z:
                k = kz_ref[row - n_x].astype(jnp.float32)
            else:
                q = row - n_x - n_z
                k = float(q + 1 if q < 8 else 8 * (q - 7))
            kb_ref[row : row + 1, :] = jnp.full((1, LANES), k, jnp.float32)

    for frame in range(frames_here):
        counts = [counts_ref[frame, brick ^ d] for d in ids]
        starts = [jnp.int32(0)]
        for count in counts:
            starts.append(starts[-1] + (count + LANES - 1) // LANES)

        def build(item, slot, frame=frame, counts=counts, starts=starts):
            shard, start, count = jnp.int32(0), starts[0], counts[0]
            for s in range(1, n_shards):
                later = item >= starts[s]
                shard = jnp.where(later, s, shard)
                start = jnp.where(later, starts[s], start)
                count = jnp.where(later, counts[s], count)
            offset = (item - start) * LANES
            where = pl.ds(pl.multiple_of(jnp.minimum(offset, capacity - LANES), LANES), LANES)
            x = pos_ref[low + shard, 0, pl.ds(frame, 1), where]
            y = pos_ref[low + shard, 1, pl.ds(frame, 1), where]
            z = pos_ref[low + shard, 2, pl.ds(frame, 1), where]
            cx, sx = cis(kb_ref[0:n_x, :] * x)
            cz, sz = cis(kb_ref[n_x : n_x + n_z, :] * z)
            cy, sy = cis(kb_ref[n_x + n_z : n_x + n_z + 16, :] * y)
            live = lane + offset < count
            cz = jnp.where(live, cz, 0.0)
            sz = jnp.where(live, sz, 0.0)
            to = pl.ds(pl.multiple_of(item * LANES, LANES), LANES)
            half = n_x + 8
            base = slot * 2 * half
            row_ref[base : base + half, :] = jnp.concatenate([cx, cy[8:16]], axis=0)
            row_ref[base + half : base + 2 * half, :] = jnp.concatenate([sx, sy[8:16]], axis=0)

            def spread(q):
                return (
                    row_ref[pl.ds(base + q, 8, stride=0), :],
                    row_ref[pl.ds(base + half + q, 8, stride=0), :],
                )

            for i in range(0, n_x, 2):
                re, im = [], []
                for q in (i, i + 1):
                    a, b = spread(q)
                    re.append(a * cz - b * sz)
                    im.append(b * cz + a * sz)
                at = i * n_z
                left_ref[at : at + 2 * n_z, to] = jnp.concatenate(re, axis=0).astype(jnp.bfloat16)
                at += rows
                left_ref[at : at + 2 * n_z, to] = jnp.concatenate(im, axis=0).astype(jnp.bfloat16)
            ce, se = cy[0:8], sy[0:8]
            re, im = [ce], [se]
            for q in range(7):
                a, b = spread(n_x + q)
                re.append(a * ce - b * se)
                im.append(b * ce + a * se)
            for q in range(0, 8, 2):
                right_ref[8 * q : 8 * q + 16, to] = jnp.concatenate(re[q : q + 2], axis=0).astype(jnp.bfloat16)
                right_ref[KMAX + 8 * q : KMAX + 8 * q + 16, to] = jnp.concatenate(im[q : q + 2], axis=0).astype(jnp.bfloat16)

        def build_unit(at_unit, carry, build=build):
            for g in range(unit):
                build(at_unit * unit + g, g)
            return carry

        units = (starts[-1] + unit - 1) // unit
        lax.fori_loop(0, units, build_unit, 0)
        prod_ref = outs[0].at[frame] if not last else outs[-1].at[frame]
        prod_ref[...] = jnp.zeros(prod_ref.shape, jnp.float32) if first else prod_in[frame]

        def multiply(width):
            def step(base):
                where = pl.ds(pl.multiple_of(base, unit * LANES), width)
                prod_ref[...] += lax.dot_general(
                    left_ref[:, where],
                    right_ref[:, where],
                    (((1,), (1,)), ((), ())),
                    preferred_element_type=jnp.float32,
                )

            return step

        wide = multiply(BIG * unit * LANES)
        full = units // BIG

        def wide_step(i, carry, wide=wide):
            wide(i * (BIG * unit * LANES))
            return carry

        lax.fori_loop(0, full, wide_step, 0)
        for rest in range(1, BIG):

            @pl.when(units - full * BIG == rest)
            def _(rest=rest, multiply=multiply, full=full):
                multiply(rest * unit * LANES)(full * (BIG * unit * LANES))

    if last:
        copies[0].wait()
        send_own_rows(outs, groups, rows, share, frames_here, local[0])


def send_own_rows(outs, groups, rows, share, frames_here, ky_ref):
    prods = outs[-1]
    width = groups * share
    group = lax.axis_index("frames")
    column = lax.broadcasted_iota(jnp.int32, (1, width), 1)
    parts = [
        jnp.where(column == dest * share + j, ky_ref[(group ^ dest) * share + j], 0)
        for dest in range(groups)
        for j in range(share)
    ]
    while len(parts) > 1:
        parts = [sum(parts[i : i + 2][1:], parts[i]) for i in range(0, len(parts), 2)]
    wanted = parts[0]
    ks = lax.broadcasted_iota(jnp.int32, (KMAX, width), 0) + 1
    hot = jnp.where(ks == wanted, 1.0, 0.0).astype(jnp.bfloat16)
    none = jnp.zeros_like(hot)
    hot = jnp.concatenate(
        [jnp.concatenate([hot, none], axis=1), jnp.concatenate([none, hot], axis=1)], axis=0
    )
    hot = jnp.concatenate([hot, hot, hot], axis=0)
    first_half = lax.broadcasted_iota(jnp.int32, (rows, 2 * KMAX), 1) < KMAX
    for frame in range(frames_here):
        top = prods[frame, 0:rows, :]
        low = pltpu.roll(prods[frame, rows : 2 * rows, :], KMAX, 1)
        terms = jnp.where(first_half, top - low, -(top + low))
        hi = terms.astype(jnp.bfloat16)
        rest = terms - hi.astype(jnp.float32)
        mid = rest.astype(jnp.bfloat16)
        tail = (rest - mid.astype(jnp.float32)).astype(jnp.bfloat16)
        split = jnp.concatenate([hi, mid, tail], axis=1)
        picked = lax.dot_general(
            hot, split, (((0,), (1,)), ((), ())), preferred_element_type=jnp.float32
        )
        for part in range(2):
            for dest in range(groups):
                at = part * width + dest * share
                to = (frame * 2 + part) * share
                outs[dest][to : to + share, :] = picked[at : at + share, :]


def dft_table(table_ref, frames_total, atoms):
    weights = [0.5 - 0.5 * math.cos(2.0 * math.pi * (t + 0.5) / frames_total) for t in range(frames_total)]
    scale = 1.0 / math.sqrt(atoms * sum(w * w for w in weights))
    shape = (2 * frames_total, NW)
    row = lax.broadcasted_iota(jnp.int32, shape, 0)
    time = row // 2
    real = row % 2 == 0
    freq = lax.broadcasted_iota(jnp.int32, shape, 1)
    window = 0.5 - 0.5 * cis((time.astype(jnp.float32) + 0.5) / frames_total)[0]
    c, s = cis((time * freq % NW).astype(jnp.float32) / NW)
    cw, sw = scale * window * c, scale * window * s
    full = jnp.concatenate([jnp.where(real, cw, sw), jnp.where(real, -sw, cw)], axis=1)
    hi = full.astype(jnp.bfloat16)
    lo = (full - hi.astype(jnp.float32)).astype(jnp.bfloat16)
    none = jnp.zeros_like(hi)
    size = 2 * frames_total
    for split, part in enumerate((hi, lo, hi)):
        at = split * 2 * size
        table_ref[at : at + size, :] = jnp.concatenate([part, none], axis=1)
        table_ref[at + size : at + 2 * size, :] = jnp.concatenate([none, part], axis=1)


def spectrum_kernel(groups, share, chunk, n_x, n_z, frames_total, atoms, *refs):
    srcs = refs[:groups]
    out_hbm, out_ref, all_ref, table_ref, sem = refs[groups:]
    block = srcs[0].shape[0]
    terms = groups * block // share
    rows = n_x * n_z
    for distance in range(groups):
        at = pl.multiple_of((lax.axis_index("frames") ^ distance) * block, block)
        all_ref[pl.ds(at, block), :] = srcs[distance][...]
    dft_table(table_ref, frames_total, atoms)

    copies = []
    for base in range(0, share, chunk):
        for first in range(base, base + chunk, 2 * PAIRS):
            stacks = []
            for j in range(first, first + 2 * PAIRS, 2):
                x = jnp.concatenate(
                    [all_ref[pl.ds(j + q, terms, stride=share), :] for q in range(2)], axis=0
                )
                hi = x.astype(jnp.bfloat16)
                lo = (x - hi.astype(jnp.float32)).astype(jnp.bfloat16)
                stacks.append(jnp.concatenate([hi, hi, lo], axis=0))
            y = lax.dot_general(
                jnp.concatenate(stacks, axis=1),
                table_ref[...],
                (((0,), (0,)), ((), ())),
                preferred_element_type=jnp.float32,
            )
            for q in range(2 * PAIRS):
                own = y[q // 2 * rows : (q // 2 + 1) * rows]
                at = q % 2 * 2 * NW
                re, im = own[:, at : at + NW], own[:, at + NW : at + 2 * NW]
                out_ref[:, first + q] = (re * re + im * im).reshape(n_x, n_z, NW)
        part = pl.ds(base, chunk)
        copies.append(
            pltpu.make_async_copy(
                out_ref.at[:, part], out_hbm.at[:, part], sem.at[base // chunk]
            )
        )
        copies[-1].start()
    for copy in copies:
        copy.wait()


def swap(value, axis, size, distance):
    return lax.ppermute(value, axis, [(i, i ^ distance) for i in range(size)])


def per_device(positions, counts, kvec_x, kvec_y, kvec_z):
    groups = lax.axis_size("frames")
    bricks = lax.axis_size("bricks")
    frames_here, capacity = positions.shape[1], positions.shape[2]
    n_x, n_z = kvec_x.shape[0] // bricks, kvec_z.shape[0]
    rows = n_x * n_z
    share = kvec_y.shape[0] // groups
    block = frames_here * 2 * share
    vmem = pl.BlockSpec(memory_space=pltpu.VMEM)
    prods_shape = (frames_here, 2 * rows, 2 * KMAX)
    waves_shape = (n_x + n_z + 16, LANES)
    hbm = pl.BlockSpec(memory_space=pltpu.HBM)
    smem = pl.BlockSpec(memory_space=pltpu.SMEM)

    def density(shards, low, ids, sums, last):
        first = sums is None
        unit = UNIT if len(ids) > 1 else UNIT // 2
        lanes = -(-len(ids) * capacity // (BIG * unit * LANES)) * BIG * unit * LANES
        args = [counts, kvec_x, kvec_z] if first else [kvec_y] if last else []
        args = [pltpu.with_memory_space_constraint(arg, pltpu.HBM) for arg in args]
        scratch = [pltpu.SMEM(arg.shape, jnp.int32) for arg in args[:3]]
        scratch += [
            pltpu.VMEM((2 * rows, lanes), jnp.bfloat16),
            pltpu.VMEM((2 * KMAX, lanes), jnp.bfloat16),
            pltpu.VMEM((unit * 2 * (n_x + 8), LANES), jnp.float32),
            pltpu.SemaphoreType.DMA((4,)),
        ]
        if last:
            out_shape = [jax.ShapeDtypeStruct((block, rows), jnp.float32)] * groups
            scratch = [pltpu.VMEM(prods_shape, jnp.float32)] + scratch
        else:
            out_shape = [jax.ShapeDtypeStruct(prods_shape, jnp.float32)]
            if first:
                out_shape.append(jax.ShapeDtypeStruct(waves_shape, jnp.float32))
                out_shape.append(jax.ShapeDtypeStruct(counts.shape, jnp.int32))
        atoms = frames_here * len(ids) * capacity
        return pl.pallas_call(
            functools.partial(density_kernel, unit, low, ids, first, last, groups, n_x, n_z, share),
            out_shape=out_shape,
            in_specs=[hbm] * len(args) + [vmem] * (1 if first else 3) + ([] if first else [smem]),
            out_specs=[vmem, vmem, smem] if first else [vmem] * len(out_shape),
            scratch_shapes=scratch,
            cost_estimate=pl.CostEstimate(
                flops=atoms * rows * KMAX * 8, bytes_accessed=atoms * 12, transcendentals=0
            ),
            compiler_params=pltpu.CompilerParams(vmem_limit_bytes=48 << 20),
            name="density",
        )(*args, shards, *([] if first else sums))

    held, ids, done, sums = positions[None], [0], 0, None
    distance = bricks // 2
    while distance:
        got = swap(held, "bricks", bricks, distance)
        upto = len(ids) if distance == 1 else len(ids) // 2
        if upto > done:
            out = density(held, done, ids[done:upto], sums, False)
            if sums is None:
                fixed = out[1:]
            got, prods = lax.optimization_barrier((got, out[0]))
            sums, done = (prods, *fixed), upto
        new = [i ^ distance for i in ids]
        ids = ids + new
        distance //= 2
        if distance:
            held = jnp.concatenate([held, got], axis=0)
    sends = density(got, 0, new, sums, True)
    got = [sends[0]] + [swap(sends[d], "frames", groups, d) for d in range(1, groups)]

    chunk = min(8, share)
    frames_total = frames_here * groups
    return pl.pallas_call(
        functools.partial(
            spectrum_kernel, groups, share, chunk, n_x, n_z, frames_total, capacity * bricks
        ),
        out_shape=jax.ShapeDtypeStruct((n_x, share, n_z, NW), jnp.float32),
        in_specs=[vmem] * groups,
        out_specs=hbm,
        scratch_shapes=[
            pltpu.VMEM((n_x, share, n_z, NW), jnp.float32),
            pltpu.VMEM((groups * block, rows), jnp.float32),
            pltpu.VMEM((12 * frames_total, 4 * NW), jnp.bfloat16),
            pltpu.SemaphoreType.DMA((share // chunk,)),
        ],
        compiler_params=pltpu.CompilerParams(vmem_limit_bytes=16 << 20),
        name="spectrum",
    )(*got)


def solution(mesh):
    return jax.shard_map(
        per_device,
        mesh=mesh,
        in_specs=(P(None, "frames", "bricks"), P("frames", None), P(), P(), P()),
        out_specs=P("bricks", "frames", None, None),
        check_vma=False,
    )
```

```python
import functools
import math

import jax
import jax.numpy as jnp
import numpy as np
from jax import lax
from jax.experimental import pallas as pl
from jax.experimental.pallas import tpu as pltpu
from jax.sharding import PartitionSpec as P

NW = 128
KMAX = 64
LANES = 128
UNIT = 4
PAIRS = 2
BIG = 8

def _fit(fun, degree):
    nodes = 0.125 * (1.0 + np.cos(np.pi * (np.arange(64) + 0.5) / 64))
    series = np.polynomial.chebyshev.Chebyshev.fit(nodes, fun(np.sqrt(nodes)), degree, domain=[0.0, 0.25])
    return [float(c) for c in series.convert(kind=np.polynomial.Polynomial).coef]


COS_C = _fit(lambda f: math.sqrt(2.0) * np.cos(np.pi * f), 4)
SIN_C = _fit(lambda f: math.sqrt(2.0) * np.sin(np.pi * f) / f, 4)


def _poly(coefs, u):
    acc = coefs[-1] * u + coefs[-2]
    for c in coefs[-3::-1]:
        acc = acc * u + c
    return acc


def cis(turns):
    f = turns - jnp.round(turns)
    u = f * f
    half_c = _poly(COS_C, u)
    half_s = _poly(SIN_C, u) * f
    return 1.0 - half_s * half_s, half_s * half_c


def density_kernel(unit, ids, first, last, groups, n_x, n_z, share, *refs):
    n_args = 4 if first else 1 if last else 0
    args, refs = refs[:n_args], refs[n_args:]
    left_ref, right_ref, row_ref, arg_sem = refs[-4:]
    refs = refs[:-4]
    if not first:
        (pos_ref, prod_in, kb_ref, counts_ref), refs = refs[:4], refs[4:]
    n_local = min(n_args, 3)
    outs, local = refs[: len(refs) - n_local], refs[len(refs) - n_local :]
    if first:
        local = (*local, outs[3])
    copies = [
        pltpu.make_async_copy(args[i], local[i], arg_sem.at[i]) for i in range(n_args)
    ]
    for copy in copies:
        copy.start()
    if first:
        counts_ref, pos_ref, kb_ref = local[0], local[3], outs[1]
    rows = n_x * n_z
    n_shards, _, frames_here, capacity = pos_ref.shape
    brick = lax.axis_index("bricks")
    lane = lax.broadcasted_iota(jnp.int32, (n_z, LANES), 1)

    if first:
        kx_ref, kz_ref = local[1:3]
        copies[0].wait()
        for frame in range(frames_here):
            for at in range(counts_ref.shape[1]):
                outs[2][frame, at] = counts_ref[frame, at]
        copies[1].wait()
        copies[2].wait()
        for row in range(n_x + n_z + 16):
            if row < n_x:
                k = kx_ref[brick * n_x + row].astype(jnp.float32)
            elif row < n_x + n_z:
                k = kz_ref[row - n_x].astype(jnp.float32)
            else:
                q = row - n_x - n_z
                k = float(q + 1 if q < 8 else 8 * (q - 7))
            kb_ref[row : row + 1, :] = jnp.full((1, LANES), k, jnp.float32)
        copies[3].wait()

    for frame in range(frames_here):
        counts = [counts_ref[frame, brick ^ d] for d in ids]
        starts = [jnp.int32(0)]
        for count in counts:
            starts.append(starts[-1] + (count + LANES - 1) // LANES)

        def build(item, slot, frame=frame, counts=counts, starts=starts):
            shard, start, count = jnp.int32(0), starts[0], counts[0]
            for s in range(1, n_shards):
                later = item >= starts[s]
                shard = jnp.where(later, s, shard)
                start = jnp.where(later, starts[s], start)
                count = jnp.where(later, counts[s], count)
            offset = (item - start) * LANES
            where = pl.ds(pl.multiple_of(jnp.minimum(offset, capacity - LANES), LANES), LANES)
            x = pos_ref[shard, 0, pl.ds(frame, 1), where]
            y = pos_ref[shard, 1, pl.ds(frame, 1), where]
            z = pos_ref[shard, 2, pl.ds(frame, 1), where]
            cx, sx = cis(kb_ref[0:n_x, :] * x)
            cz, sz = cis(kb_ref[n_x : n_x + n_z, :] * z)
            cy, sy = cis(kb_ref[n_x + n_z : n_x + n_z + 16, :] * y)
            live = lane + offset < count
            cz = jnp.where(live, cz, 0.0)
            sz = jnp.where(live, sz, 0.0)
            to = pl.ds(pl.multiple_of(item * LANES, LANES), LANES)
            half = n_x + 8
            base = slot * 2 * half
            row_ref[base : base + half, :] = jnp.concatenate([cx, cy[8:16]], axis=0)
            row_ref[base + half : base + 2 * half, :] = jnp.concatenate([sx, sy[8:16]], axis=0)

            def spread(q):
                return (
                    row_ref[pl.ds(base + q, 8, stride=0), :],
                    row_ref[pl.ds(base + half + q, 8, stride=0), :],
                )

            for i in range(0, n_x, 2):
                re, im = [], []
                for q in (i, i + 1):
                    a, b = spread(q)
                    re.append(a * cz - b * sz)
                    im.append(b * cz + a * sz)
                at = i * n_z
                left_ref[at : at + 2 * n_z, to] = jnp.concatenate(re, axis=0).astype(jnp.bfloat16)
                at += rows
                left_ref[at : at + 2 * n_z, to] = jnp.concatenate(im, axis=0).astype(jnp.bfloat16)
            ce, se = cy[0:8], sy[0:8]
            re, im = [ce], [se]
            for q in range(7):
                a, b = spread(n_x + q)
                re.append(a * ce - b * se)
                im.append(b * ce + a * se)
            for q in range(0, 8, 2):
                right_ref[8 * q : 8 * q + 16, to] = jnp.concatenate(re[q : q + 2], axis=0).astype(jnp.bfloat16)
                right_ref[KMAX + 8 * q : KMAX + 8 * q + 16, to] = jnp.concatenate(im[q : q + 2], axis=0).astype(jnp.bfloat16)

        def build_unit(at_unit, carry, build=build):
            for g in range(unit):
                build(at_unit * unit + g, g)
            return carry

        units = (starts[-1] + unit - 1) // unit
        lax.fori_loop(0, units, build_unit, 0)
        prod_ref = outs[0].at[frame] if not last else outs[-1].at[frame]
        prod_ref[...] = jnp.zeros(prod_ref.shape, jnp.float32) if first else prod_in[frame]

        def multiply(width):
            def step(base):
                where = pl.ds(pl.multiple_of(base, unit * LANES), width)
                prod_ref[...] += lax.dot_general(
                    left_ref[:, where],
                    right_ref[:, where],
                    (((1,), (1,)), ((), ())),
                    preferred_element_type=jnp.float32,
                )

            return step

        wide = multiply(BIG * unit * LANES)
        full = units // BIG

        def wide_step(i, carry, wide=wide):
            wide(i * (BIG * unit * LANES))
            return carry

        lax.fori_loop(0, full, wide_step, 0)
        for rest in range(1, BIG):

            @pl.when(units - full * BIG == rest)
            def _(rest=rest, multiply=multiply, full=full):
                multiply(rest * unit * LANES)(full * (BIG * unit * LANES))

    if last:
        copies[0].wait()
        send_own_rows(outs, groups, rows, share, frames_here, local[0])


def send_own_rows(outs, groups, rows, share, frames_here, ky_ref):
    prods = outs[-1]
    width = groups * share
    group = lax.axis_index("frames")
    column = lax.broadcasted_iota(jnp.int32, (1, width), 1)
    parts = [
        jnp.where(column == dest * share + j, ky_ref[(group ^ dest) * share + j], 0)
        for dest in range(groups)
        for j in range(share)
    ]
    while len(parts) > 1:
        parts = [sum(parts[i : i + 2][1:], parts[i]) for i in range(0, len(parts), 2)]
    wanted = parts[0]
    ks = lax.broadcasted_iota(jnp.int32, (KMAX, width), 0) + 1
    hot = jnp.where(ks == wanted, 1.0, 0.0).astype(jnp.bfloat16)
    none = jnp.zeros_like(hot)
    hot = jnp.concatenate(
        [jnp.concatenate([hot, none], axis=1), jnp.concatenate([none, hot], axis=1)], axis=0
    )
    hot = jnp.concatenate([hot, hot, hot], axis=0)
    first_half = lax.broadcasted_iota(jnp.int32, (rows, 2 * KMAX), 1) < KMAX
    for frame in range(frames_here):
        top = prods[frame, 0:rows, :]
        low = pltpu.roll(prods[frame, rows : 2 * rows, :], KMAX, 1)
        terms = jnp.where(first_half, top - low, -(top + low))
        hi = terms.astype(jnp.bfloat16)
        rest = terms - hi.astype(jnp.float32)
        mid = rest.astype(jnp.bfloat16)
        tail = (rest - mid.astype(jnp.float32)).astype(jnp.bfloat16)
        split = jnp.concatenate([hi, mid, tail], axis=1)
        picked = lax.dot_general(
            hot, split, (((0,), (1,)), ((), ())), preferred_element_type=jnp.float32
        )
        for part in range(2):
            for dest in range(groups):
                at = part * width + dest * share
                to = (frame * 2 + part) * share
                outs[dest][to : to + share, :] = picked[at : at + share, :]


def dft_table(table_ref, frames_total, atoms):
    weights = [0.5 - 0.5 * math.cos(2.0 * math.pi * (t + 0.5) / frames_total) for t in range(frames_total)]
    scale = 1.0 / math.sqrt(atoms * sum(w * w for w in weights))
    shape = (2 * frames_total, NW)
    row = lax.broadcasted_iota(jnp.int32, shape, 0)
    time = row // 2
    real = row % 2 == 0
    freq = lax.broadcasted_iota(jnp.int32, shape, 1)
    window = 0.5 - 0.5 * cis((time.astype(jnp.float32) + 0.5) / frames_total)[0]
    c, s = cis((time * freq % NW).astype(jnp.float32) / NW)
    cw, sw = scale * window * c, scale * window * s
    full = jnp.concatenate([jnp.where(real, cw, sw), jnp.where(real, -sw, cw)], axis=1)
    hi = full.astype(jnp.bfloat16)
    lo = (full - hi.astype(jnp.float32)).astype(jnp.bfloat16)
    none = jnp.zeros_like(hi)
    size = 2 * frames_total
    for split, part in enumerate((hi, lo, hi)):
        at = split * 2 * size
        table_ref[at : at + size, :] = jnp.concatenate([part, none], axis=1)
        table_ref[at + size : at + 2 * size, :] = jnp.concatenate([none, part], axis=1)


def spectrum_kernel(groups, share, chunk, n_x, n_z, frames_total, atoms, *refs):
    srcs = refs[:groups]
    out_hbm, out_ref, all_ref, table_ref, sem = refs[groups:]
    block = srcs[0].shape[0]
    terms = groups * block // share
    rows = n_x * n_z
    for distance in range(groups):
        at = pl.multiple_of((lax.axis_index("frames") ^ distance) * block, block)
        all_ref[pl.ds(at, block), :] = srcs[distance][...]
    dft_table(table_ref, frames_total, atoms)

    copies = []
    for base in range(0, share, chunk):
        for first in range(base, base + chunk, 2 * PAIRS):
            stacks = []
            for j in range(first, first + 2 * PAIRS, 2):
                x = jnp.concatenate(
                    [all_ref[pl.ds(j + q, terms, stride=share), :] for q in range(2)], axis=0
                )
                hi = x.astype(jnp.bfloat16)
                lo = (x - hi.astype(jnp.float32)).astype(jnp.bfloat16)
                stacks.append(jnp.concatenate([hi, hi, lo], axis=0))
            y = lax.dot_general(
                jnp.concatenate(stacks, axis=1),
                table_ref[...],
                (((0,), (0,)), ((), ())),
                preferred_element_type=jnp.float32,
            )
            for q in range(2 * PAIRS):
                own = y[q // 2 * rows : (q // 2 + 1) * rows]
                at = q % 2 * 2 * NW
                re, im = own[:, at : at + NW], own[:, at + NW : at + 2 * NW]
                out_ref[:, first + q] = (re * re + im * im).reshape(n_x, n_z, NW)
        part = pl.ds(base, chunk)
        copies.append(
            pltpu.make_async_copy(
                out_ref.at[:, part], out_hbm.at[:, part], sem.at[base // chunk]
            )
        )
        copies[-1].start()
    for copy in copies:
        copy.wait()


def swap(value, axis, size, distance):
    return lax.ppermute(value, axis, [(i, i ^ distance) for i in range(size)])


def per_device(positions, counts, kvec_x, kvec_y, kvec_z):
    groups = lax.axis_size("frames")
    bricks = lax.axis_size("bricks")
    frames_here, capacity = positions.shape[1], positions.shape[2]
    n_x, n_z = kvec_x.shape[0] // bricks, kvec_z.shape[0]
    rows = n_x * n_z
    share = kvec_y.shape[0] // groups
    block = frames_here * 2 * share
    vmem = pl.BlockSpec(memory_space=pltpu.VMEM)
    prods_shape = (frames_here, 2 * rows, 2 * KMAX)
    waves_shape = (n_x + n_z + 16, LANES)
    hbm = pl.BlockSpec(memory_space=pltpu.HBM)
    smem = pl.BlockSpec(memory_space=pltpu.SMEM)

    def density(shards, ids, sums, last):
        first = sums is None
        unit = UNIT if len(ids) > 1 else UNIT // 2
        lanes = -(-len(ids) * capacity // (BIG * unit * LANES)) * BIG * unit * LANES
        args = [counts, kvec_x, kvec_z, shards] if first else [kvec_y] if last else []
        args = [pltpu.with_memory_space_constraint(arg, pltpu.HBM) for arg in args]
        scratch = [pltpu.SMEM(arg.shape, jnp.int32) for arg in args[:3]]
        scratch += [
            pltpu.VMEM((2 * rows, lanes), jnp.bfloat16),
            pltpu.VMEM((2 * KMAX, lanes), jnp.bfloat16),
            pltpu.VMEM((unit * 2 * (n_x + 8), LANES), jnp.float32),
            pltpu.SemaphoreType.DMA((4,)),
        ]
        if last:
            out_shape = [jax.ShapeDtypeStruct((block, rows), jnp.float32)] * groups
            scratch = [pltpu.VMEM(prods_shape, jnp.float32)] + scratch
        else:
            out_shape = [jax.ShapeDtypeStruct(prods_shape, jnp.float32)]
            if first:
                out_shape.append(jax.ShapeDtypeStruct(waves_shape, jnp.float32))
                out_shape.append(jax.ShapeDtypeStruct(counts.shape, jnp.int32))
                out_shape.append(jax.ShapeDtypeStruct(shards.shape, jnp.float32))
        atoms = frames_here * len(ids) * capacity
        return pl.pallas_call(
            functools.partial(density_kernel, unit, ids, first, last, groups, n_x, n_z, share),
            out_shape=out_shape,
            in_specs=[hbm] * len(args) + ([] if first else [vmem] * 3 + [smem]),
            out_specs=[vmem, vmem, smem, vmem] if first else [vmem] * len(out_shape),
            scratch_shapes=scratch,
            cost_estimate=pl.CostEstimate(
                flops=atoms * rows * KMAX * 8, bytes_accessed=atoms * 12, transcendentals=0
            ),
            compiler_params=pltpu.CompilerParams(vmem_limit_bytes=48 << 20),
            name="density",
        )(*args, *([] if first else [shards, *sums]))

    held, fresh, ids = positions[None], positions[None], [0]
    new, sums, fixed = [0], None, None
    distance = bricks // 2
    while distance:
        got = swap(held, "bricks", bricks, distance)
        out = density(fresh, new, sums, False)
        if sums is None:
            fixed, held = out[1:3], out[3]
        got, prods = lax.optimization_barrier((got, out[0]))
        sums = (prods, *fixed)
        new = [i ^ distance for i in ids]
        ids, fresh = ids + new, got
        distance //= 2
        if distance:
            held = jnp.concatenate([held, got], axis=0)
    sends = density(fresh, new, sums, True)
    got = [sends[0]] + [swap(sends[d], "frames", groups, d) for d in range(1, groups)]

    chunk = min(8, share)
    frames_total = frames_here * groups
    return pl.pallas_call(
        functools.partial(
            spectrum_kernel, groups, share, chunk, n_x, n_z, frames_total, capacity * bricks
        ),
        out_shape=jax.ShapeDtypeStruct((n_x, share, n_z, NW), jnp.float32),
        in_specs=[vmem] * groups,
        out_specs=hbm,
        scratch_shapes=[
            pltpu.VMEM((n_x, share, n_z, NW), jnp.float32),
            pltpu.VMEM((groups * block, rows), jnp.float32),
            pltpu.VMEM((12 * frames_total, 4 * NW), jnp.bfloat16),
            pltpu.SemaphoreType.DMA((share // chunk,)),
        ],
        compiler_params=pltpu.CompilerParams(vmem_limit_bytes=16 << 20),
        name="spectrum",
    )(*got)


def solution(mesh):
    return jax.shard_map(
        per_device,
        mesh=mesh,
        in_specs=(P(None, "frames", "bricks"), P("frames", None), P(), P(), P()),
        out_specs=P("bricks", "frames", None, None),
        check_vma=False,
    )
```

```python
import functools
import math

import jax
import jax.numpy as jnp
import numpy as np
from jax import lax
from jax.experimental import pallas as pl
from jax.experimental.pallas import tpu as pltpu
from jax.sharding import PartitionSpec as P

NW = 128
KMAX = 64
LANES = 128
UNIT = 4
PAIRS = 2
BIG = 8

def _fit(fun, degree):
    nodes = 0.125 * (1.0 + np.cos(np.pi * (np.arange(64) + 0.5) / 64))
    series = np.polynomial.chebyshev.Chebyshev.fit(nodes, fun(np.sqrt(nodes)), degree, domain=[0.0, 0.25])
    return [float(c) for c in series.convert(kind=np.polynomial.Polynomial).coef]


COS_C = _fit(lambda f: math.sqrt(2.0) * np.cos(np.pi * f), 4)
SIN_C = _fit(lambda f: math.sqrt(2.0) * np.sin(np.pi * f) / f, 4)


def _poly(coefs, u):
    acc = coefs[-1] * u + coefs[-2]
    for c in coefs[-3::-1]:
        acc = acc * u + c
    return acc


def cis(turns):
    f = turns - jnp.round(turns)
    u = f * f
    half_c = _poly(COS_C, u)
    half_s = _poly(SIN_C, u) * f
    return 1.0 - half_s * half_s, half_s * half_c


def density_kernel(unit, ids, first, last, groups, n_x, n_z, share, *refs):
    n_args = 4 if first else 1 if last else 0
    args, refs = refs[:n_args], refs[n_args:]
    left_ref, right_ref, row_ref, arg_sem = refs[-4:]
    refs = refs[:-4]
    if not first:
        (pos_ref, prod_in, kb_ref, counts_ref), refs = refs[:4], refs[4:]
    n_local = min(n_args, 3)
    outs, local = refs[: len(refs) - n_local], refs[len(refs) - n_local :]
    if first:
        local = (*local, outs[3])
    copies = [
        pltpu.make_async_copy(args[i], local[i], arg_sem.at[i]) for i in range(n_args)
    ]
    for copy in copies:
        copy.start()
    if first:
        counts_ref, pos_ref, kb_ref = local[0], local[3], outs[1]
    rows = n_x * n_z
    n_shards, _, frames_here, capacity = pos_ref.shape
    brick = lax.axis_index("bricks")
    lane = lax.broadcasted_iota(jnp.int32, (n_z, LANES), 1)

    if first:
        kx_ref, kz_ref = local[1:3]
        copies[0].wait()
        for frame in range(frames_here):
            for at in range(counts_ref.shape[1]):
                outs[2][frame, at] = counts_ref[frame, at]
        copies[1].wait()
        copies[2].wait()
        for row in range(n_x + n_z + 16):
            if row < n_x:
                k = kx_ref[brick * n_x + row].astype(jnp.float32)
            elif row < n_x + n_z:
                k = kz_ref[row - n_x].astype(jnp.float32)
            else:
                q = row - n_x - n_z
                k = float(q + 1 if q < 8 else 8 * (q - 7))
            kb_ref[row : row + 1, :] = jnp.full((1, LANES), k, jnp.float32)
        copies[3].wait()

    for frame in range(frames_here):
        counts = [counts_ref[frame, brick ^ d] for d in ids]
        starts = [jnp.int32(0)]
        for count in counts:
            starts.append(starts[-1] + (count + LANES - 1) // LANES)

        def build(item, slot, frame=frame, counts=counts, starts=starts):
            shard, start, count = jnp.int32(0), starts[0], counts[0]
            for s in range(1, n_shards):
                later = item >= starts[s]
                shard = jnp.where(later, s, shard)
                start = jnp.where(later, starts[s], start)
                count = jnp.where(later, counts[s], count)
            offset = (item - start) * LANES
            where = pl.ds(pl.multiple_of(jnp.minimum(offset, capacity - LANES), LANES), LANES)
            x = pos_ref[shard, 0, pl.ds(frame, 1), where]
            y = pos_ref[shard, 1, pl.ds(frame, 1), where]
            z = pos_ref[shard, 2, pl.ds(frame, 1), where]
            cx, sx = cis(kb_ref[0:n_x, :] * x)
            cz, sz = cis(kb_ref[n_x : n_x + n_z, :] * z)
            cy, sy = cis(kb_ref[n_x + n_z : n_x + n_z + 16, :] * y)
            live = lane + offset < count
            cz = jnp.where(live, cz, 0.0)
            sz = jnp.where(live, sz, 0.0)
            to = pl.ds(pl.multiple_of(item * LANES, LANES), LANES)
            half = n_x + 8
            base = slot * 2 * half
            row_ref[base : base + half, :] = jnp.concatenate([cx, cy[8:16]], axis=0)
            row_ref[base + half : base + 2 * half, :] = jnp.concatenate([sx, sy[8:16]], axis=0)

            def spread(q):
                return (
                    row_ref[pl.ds(base + q, 8, stride=0), :],
                    row_ref[pl.ds(base + half + q, 8, stride=0), :],
                )

            for i in range(0, n_x, 2):
                re, im = [], []
                for q in (i, i + 1):
                    a, b = spread(q)
                    re.append(a * cz - b * sz)
                    im.append(b * cz + a * sz)
                at = i * n_z
                left_ref[at : at + 2 * n_z, to] = jnp.concatenate(re, axis=0).astype(jnp.bfloat16)
                at += rows
                left_ref[at : at + 2 * n_z, to] = jnp.concatenate(im, axis=0).astype(jnp.bfloat16)
            ce, se = cy[0:8], sy[0:8]
            re, im = [ce], [se]
            for q in range(7):
                a, b = spread(n_x + q)
                re.append(a * ce - b * se)
                im.append(b * ce + a * se)
            for q in range(0, 8, 2):
                right_ref[8 * q : 8 * q + 16, to] = jnp.concatenate(re[q : q + 2], axis=0).astype(jnp.bfloat16)
                right_ref[KMAX + 8 * q : KMAX + 8 * q + 16, to] = jnp.concatenate(im[q : q + 2], axis=0).astype(jnp.bfloat16)

        def build_unit(at_unit, carry, build=build):
            for g in range(unit):
                build(at_unit * unit + g, g)
            return carry

        units = (starts[-1] + unit - 1) // unit
        lax.fori_loop(0, units, build_unit, 0)
        prod_ref = outs[0].at[frame] if not last else outs[-1].at[frame]
        prod_ref[...] = jnp.zeros(prod_ref.shape, jnp.float32) if first else prod_in[frame]

        def multiply(width):
            def step(base):
                where = pl.ds(pl.multiple_of(base, unit * LANES), width)
                prod_ref[...] += lax.dot_general(
                    left_ref[:, where],
                    right_ref[:, where],
                    (((1,), (1,)), ((), ())),
                    preferred_element_type=jnp.float32,
                )

            return step

        wide = multiply(BIG * unit * LANES)
        full = units // BIG

        def wide_step(i, carry, wide=wide):
            wide(i * (BIG * unit * LANES))
            return carry

        lax.fori_loop(0, full, wide_step, 0)
        for rest in range(1, BIG):

            @pl.when(units - full * BIG == rest)
            def _(rest=rest, multiply=multiply, full=full):
                multiply(rest * unit * LANES)(full * (BIG * unit * LANES))

    if last:
        copies[0].wait()
        send_own_rows(outs, groups, rows, share, frames_here, local[0])


def send_own_rows(outs, groups, rows, share, frames_here, ky_ref):
    prods = outs[-1]
    width = groups * share
    group = lax.axis_index("frames")
    column = lax.broadcasted_iota(jnp.int32, (1, width), 1)
    parts = [
        jnp.where(column == dest * share + j, ky_ref[(group ^ dest) * share + j], 0)
        for dest in range(groups)
        for j in range(share)
    ]
    while len(parts) > 1:
        parts = [sum(parts[i : i + 2][1:], parts[i]) for i in range(0, len(parts), 2)]
    wanted = parts[0]
    ks = lax.broadcasted_iota(jnp.int32, (KMAX, width), 0) + 1
    hot = jnp.where(ks == wanted, 1.0, 0.0).astype(jnp.bfloat16)
    none = jnp.zeros_like(hot)
    hot = jnp.concatenate(
        [jnp.concatenate([hot, none], axis=1), jnp.concatenate([none, hot], axis=1)], axis=0
    )
    hot = jnp.concatenate([hot, hot, hot], axis=0)
    first_half = lax.broadcasted_iota(jnp.int32, (rows, 2 * KMAX), 1) < KMAX
    for frame in range(frames_here):
        top = prods[frame, 0:rows, :]
        low = pltpu.roll(prods[frame, rows : 2 * rows, :], KMAX, 1)
        terms = jnp.where(first_half, top - low, -(top + low))
        hi = terms.astype(jnp.bfloat16)
        rest = terms - hi.astype(jnp.float32)
        mid = rest.astype(jnp.bfloat16)
        tail = (rest - mid.astype(jnp.float32)).astype(jnp.bfloat16)
        split = jnp.concatenate([hi, mid, tail], axis=1)
        picked = lax.dot_general(
            hot, split, (((0,), (1,)), ((), ())), preferred_element_type=jnp.float32
        )
        for part in range(2):
            for dest in range(groups):
                at = part * width + dest * share
                to = (frame * 2 + part) * share
                outs[dest][to : to + share, :] = picked[at : at + share, :]


def dft_table(table_ref, frames_total, atoms):
    weights = [0.5 - 0.5 * math.cos(2.0 * math.pi * (t + 0.5) / frames_total) for t in range(frames_total)]
    scale = 1.0 / math.sqrt(atoms * sum(w * w for w in weights))
    shape = (2 * frames_total, NW)
    row = lax.broadcasted_iota(jnp.int32, shape, 0)
    time = row // 2
    real = row % 2 == 0
    freq = lax.broadcasted_iota(jnp.int32, shape, 1)
    window = 0.5 - 0.5 * cis((time.astype(jnp.float32) + 0.5) / frames_total)[0]
    c, s = cis((time * freq % NW).astype(jnp.float32) / NW)
    cw, sw = scale * window * c, scale * window * s
    full = jnp.concatenate([jnp.where(real, cw, sw), jnp.where(real, -sw, cw)], axis=1)
    hi = full.astype(jnp.bfloat16)
    lo = (full - hi.astype(jnp.float32)).astype(jnp.bfloat16)
    none = jnp.zeros_like(hi)
    size = 2 * frames_total
    for split, part in enumerate((hi, lo, hi)):
        at = split * 2 * size
        table_ref[at : at + size, :] = jnp.concatenate([part, none], axis=1)
        table_ref[at + size : at + 2 * size, :] = jnp.concatenate([none, part], axis=1)


def spectrum_kernel(groups, share, chunk, n_x, n_z, frames_total, atoms, *refs):
    srcs = refs[:groups]
    out_hbm, out_ref, all_ref, table_ref, sem = refs[groups:]
    block = srcs[0].shape[0]
    terms = groups * block // share
    rows = n_x * n_z
    for distance in range(groups):
        at = pl.multiple_of((lax.axis_index("frames") ^ distance) * block, block)
        all_ref[pl.ds(at, block), :] = srcs[distance][...]
    dft_table(table_ref, frames_total, atoms)

    copies = []
    for base in range(0, share, chunk):
        for first in range(base, base + chunk, 2 * PAIRS):
            stacks = []
            for j in range(first, first + 2 * PAIRS, 2):
                x = jnp.concatenate(
                    [all_ref[pl.ds(j + q, terms, stride=share), :] for q in range(2)], axis=0
                )
                hi = x.astype(jnp.bfloat16)
                lo = (x - hi.astype(jnp.float32)).astype(jnp.bfloat16)
                stacks.append(jnp.concatenate([hi, hi, lo], axis=0))
            y = lax.dot_general(
                jnp.concatenate(stacks, axis=1),
                table_ref[...],
                (((0,), (0,)), ((), ())),
                preferred_element_type=jnp.float32,
            )
            for q in range(2 * PAIRS):
                own = y[q // 2 * rows : (q // 2 + 1) * rows]
                at = q % 2 * 2 * NW
                re, im = own[:, at : at + NW], own[:, at + NW : at + 2 * NW]
                out_ref[:, first + q] = (re * re + im * im).reshape(n_x, n_z, NW)
        part = pl.ds(base, chunk)
        copies.append(
            pltpu.make_async_copy(
                out_ref.at[:, part], out_hbm.at[:, part], sem.at[base // chunk]
            )
        )
        copies[-1].start()
    for copy in copies:
        copy.wait()


def swap(value, axis, size, distance):
    return lax.ppermute(value, axis, [(i, i ^ distance) for i in range(size)])


def per_device(positions, counts, kvec_x, kvec_y, kvec_z):
    groups = lax.axis_size("frames")
    bricks = lax.axis_size("bricks")
    frames_here, capacity = positions.shape[1], positions.shape[2]
    n_x, n_z = kvec_x.shape[0] // bricks, kvec_z.shape[0]
    rows = n_x * n_z
    share = kvec_y.shape[0] // groups
    block = frames_here * 2 * share
    vmem = pl.BlockSpec(memory_space=pltpu.VMEM)
    prods_shape = (frames_here, 2 * rows, 2 * KMAX)
    waves_shape = (n_x + n_z + 16, LANES)
    hbm = pl.BlockSpec(memory_space=pltpu.HBM)
    smem = pl.BlockSpec(memory_space=pltpu.SMEM)

    def density(shards, ids, sums, last):
        first = sums is None
        unit = UNIT if len(ids) > 2 else UNIT // 2
        lanes = -(-len(ids) * capacity // (BIG * unit * LANES)) * BIG * unit * LANES
        args = [counts, kvec_x, kvec_z, shards] if first else [kvec_y] if last else []
        args = [pltpu.with_memory_space_constraint(arg, pltpu.HBM) for arg in args]
        scratch = [pltpu.SMEM(arg.shape, jnp.int32) for arg in args[:3]]
        scratch += [
            pltpu.VMEM((2 * rows, lanes), jnp.bfloat16),
            pltpu.VMEM((2 * KMAX, lanes), jnp.bfloat16),
            pltpu.VMEM((unit * 2 * (n_x + 8), LANES), jnp.float32),
            pltpu.SemaphoreType.DMA((4,)),
        ]
        if last:
            out_shape = [jax.ShapeDtypeStruct((block, rows), jnp.float32)] * groups
            scratch = [pltpu.VMEM(prods_shape, jnp.float32)] + scratch
        else:
            out_shape = [jax.ShapeDtypeStruct(prods_shape, jnp.float32)]
            if first:
                out_shape.append(jax.ShapeDtypeStruct(waves_shape, jnp.float32))
                out_shape.append(jax.ShapeDtypeStruct(counts.shape, jnp.int32))
                out_shape.append(jax.ShapeDtypeStruct(shards.shape, jnp.float32))
        atoms = frames_here * len(ids) * capacity
        return pl.pallas_call(
            functools.partial(density_kernel, unit, ids, first, last, groups, n_x, n_z, share),
            out_shape=out_shape,
            in_specs=[hbm] * len(args) + ([] if first else [vmem] * 3 + [smem]),
            out_specs=[vmem, vmem, smem, vmem] if first else [vmem] * len(out_shape),
            scratch_shapes=scratch,
            cost_estimate=pl.CostEstimate(
                flops=atoms * rows * KMAX * 8, bytes_accessed=atoms * 12, transcendentals=0
            ),
            compiler_params=pltpu.CompilerParams(vmem_limit_bytes=48 << 20),
            name="density",
        )(*args, *([] if first else [shards, *sums]))

    held, fresh, ids = positions[None], positions[None], [0]
    new, sums, fixed = [0], None, None
    distance = bricks // 2
    while distance:
        got = swap(held, "bricks", bricks, distance)
        out = density(fresh, new, sums, False)
        if sums is None:
            fixed, held = out[1:3], out[3]
        got, prods = lax.optimization_barrier((got, out[0]))
        sums = (prods, *fixed)
        new = [i ^ distance for i in ids]
        ids, fresh = ids + new, got
        distance //= 2
        if distance:
            held = jnp.concatenate([held, got], axis=0)
    sends = density(fresh, new, sums, True)
    far = [swap(sends[d], "frames", groups, d) for d in range(groups - 1, 0, -1)]
    got = [sends[0]] + far[::-1]

    chunk = min(8, share)
    frames_total = frames_here * groups
    return pl.pallas_call(
        functools.partial(
            spectrum_kernel, groups, share, chunk, n_x, n_z, frames_total, capacity * bricks
        ),
        out_shape=jax.ShapeDtypeStruct((n_x, share, n_z, NW), jnp.float32),
        in_specs=[vmem] * groups,
        out_specs=hbm,
        scratch_shapes=[
            pltpu.VMEM((n_x, share, n_z, NW), jnp.float32),
            pltpu.VMEM((groups * block, rows), jnp.float32),
            pltpu.VMEM((12 * frames_total, 4 * NW), jnp.bfloat16),
            pltpu.SemaphoreType.DMA((share // chunk,)),
        ],
        compiler_params=pltpu.CompilerParams(vmem_limit_bytes=16 << 20),
        name="spectrum",
    )(*got)


def solution(mesh):
    return jax.shard_map(
        per_device,
        mesh=mesh,
        in_specs=(P(None, "frames", "bricks"), P("frames", None), P(), P(), P()),
        out_specs=P("bricks", "frames", None, None),
        check_vma=False,
    )
```

```python
import functools
import math

import jax
import jax.numpy as jnp
import numpy as np
from jax import lax
from jax.experimental import pallas as pl
from jax.experimental.pallas import tpu as pltpu
from jax.sharding import PartitionSpec as P

NW = 128
KMAX = 64
LANES = 128
UNIT = 4
PAIRS = 2
BIG = 8

def _fit(fun, degree):
    nodes = 0.125 * (1.0 + np.cos(np.pi * (np.arange(64) + 0.5) / 64))
    series = np.polynomial.chebyshev.Chebyshev.fit(nodes, fun(np.sqrt(nodes)), degree, domain=[0.0, 0.25])
    return [float(c) for c in series.convert(kind=np.polynomial.Polynomial).coef]


COS_C = _fit(lambda f: math.sqrt(2.0) * np.cos(np.pi * f), 4)
SIN_C = _fit(lambda f: math.sqrt(2.0) * np.sin(np.pi * f) / f, 4)


def _poly(coefs, u):
    acc = coefs[-1] * u + coefs[-2]
    for c in coefs[-3::-1]:
        acc = acc * u + c
    return acc


def cis(turns):
    f = turns - jnp.round(turns)
    u = f * f
    half_c = _poly(COS_C, u)
    half_s = _poly(SIN_C, u) * f
    return 1.0 - half_s * half_s, half_s * half_c


def density_kernel(unit, frame_ids, ids, first, last, groups, n_x, n_z, share, *refs):
    n_args = 4 if first else 1 if last else 0
    args, refs = refs[:n_args], refs[n_args:]
    left_ref, right_ref, row_ref, arg_sem = refs[-4:]
    refs = refs[:-4]
    if not first:
        (pos_ref, prod_in, kb_ref, counts_ref), refs = refs[:4], refs[4:]
    n_local = min(n_args, 3)
    outs, local = refs[: len(refs) - n_local], refs[len(refs) - n_local :]
    if first:
        local = (*local, outs[3])
    copies = [
        pltpu.make_async_copy(args[i], local[i], arg_sem.at[i]) for i in range(n_args)
    ]
    for copy in copies:
        copy.start()
    if first:
        counts_ref, pos_ref, kb_ref = local[0], local[3], outs[1]
    rows = n_x * n_z
    n_shards, _, frames_here, capacity = pos_ref.shape
    brick = lax.axis_index("bricks")
    lane = lax.broadcasted_iota(jnp.int32, (n_z, LANES), 1)

    if first:
        kx_ref, kz_ref = local[1:3]
        copies[0].wait()
        for frame in range(frames_here):
            for at in range(counts_ref.shape[1]):
                outs[2][frame, at] = counts_ref[frame, at]
        copies[1].wait()
        copies[2].wait()
        for row in range(n_x + n_z + 16):
            if row < n_x:
                k = kx_ref[brick * n_x + row].astype(jnp.float32)
            elif row < n_x + n_z:
                k = kz_ref[row - n_x].astype(jnp.float32)
            else:
                q = row - n_x - n_z
                k = float(q + 1 if q < 8 else 8 * (q - 7))
            kb_ref[row : row + 1, :] = jnp.full((1, LANES), k, jnp.float32)
        copies[3].wait()

    for frame in frame_ids:
        counts = [counts_ref[frame, brick ^ d] for d in ids]
        starts = [jnp.int32(0)]
        for count in counts:
            starts.append(starts[-1] + (count + LANES - 1) // LANES)

        def build(item, slot, frame=frame, counts=counts, starts=starts):
            shard, start, count = jnp.int32(0), starts[0], counts[0]
            for s in range(1, n_shards):
                later = item >= starts[s]
                shard = jnp.where(later, s, shard)
                start = jnp.where(later, starts[s], start)
                count = jnp.where(later, counts[s], count)
            offset = (item - start) * LANES
            where = pl.ds(pl.multiple_of(jnp.minimum(offset, capacity - LANES), LANES), LANES)
            x = pos_ref[shard, 0, pl.ds(frame, 1), where]
            y = pos_ref[shard, 1, pl.ds(frame, 1), where]
            z = pos_ref[shard, 2, pl.ds(frame, 1), where]
            cx, sx = cis(kb_ref[0:n_x, :] * x)
            cz, sz = cis(kb_ref[n_x : n_x + n_z, :] * z)
            cy, sy = cis(kb_ref[n_x + n_z : n_x + n_z + 16, :] * y)
            live = lane + offset < count
            cz = jnp.where(live, cz, 0.0)
            sz = jnp.where(live, sz, 0.0)
            to = pl.ds(pl.multiple_of(item * LANES, LANES), LANES)
            half = n_x + 8
            base = slot * 2 * half
            row_ref[base : base + half, :] = jnp.concatenate([cx, cy[8:16]], axis=0)
            row_ref[base + half : base + 2 * half, :] = jnp.concatenate([sx, sy[8:16]], axis=0)

            def spread(q):
                return (
                    row_ref[pl.ds(base + q, 8, stride=0), :],
                    row_ref[pl.ds(base + half + q, 8, stride=0), :],
                )

            for i in range(0, n_x, 2):
                re, im = [], []
                for q in (i, i + 1):
                    a, b = spread(q)
                    re.append(a * cz - b * sz)
                    im.append(b * cz + a * sz)
                at = i * n_z
                left_ref[at : at + 2 * n_z, to] = jnp.concatenate(re, axis=0).astype(jnp.bfloat16)
                at += rows
                left_ref[at : at + 2 * n_z, to] = jnp.concatenate(im, axis=0).astype(jnp.bfloat16)
            ce, se = cy[0:8], sy[0:8]
            re, im = [ce], [se]
            for q in range(7):
                a, b = spread(n_x + q)
                re.append(a * ce - b * se)
                im.append(b * ce + a * se)
            for q in range(0, 8, 2):
                right_ref[8 * q : 8 * q + 16, to] = jnp.concatenate(re[q : q + 2], axis=0).astype(jnp.bfloat16)
                right_ref[KMAX + 8 * q : KMAX + 8 * q + 16, to] = jnp.concatenate(im[q : q + 2], axis=0).astype(jnp.bfloat16)

        def build_unit(at_unit, carry, build=build):
            for g in range(unit):
                build(at_unit * unit + g, g)
            return carry

        units = (starts[-1] + unit - 1) // unit
        lax.fori_loop(0, units, build_unit, 0)
        prod_ref = outs[0].at[frame] if not last else outs[-1].at[frame]
        prod_ref[...] = jnp.zeros(prod_ref.shape, jnp.float32) if first else prod_in[frame]

        def multiply(width):
            def step(base):
                where = pl.ds(pl.multiple_of(base, unit * LANES), width)
                prod_ref[...] += lax.dot_general(
                    left_ref[:, where],
                    right_ref[:, where],
                    (((1,), (1,)), ((), ())),
                    preferred_element_type=jnp.float32,
                )

            return step

        wide = multiply(BIG * unit * LANES)
        full = units // BIG

        def wide_step(i, carry, wide=wide):
            wide(i * (BIG * unit * LANES))
            return carry

        lax.fori_loop(0, full, wide_step, 0)
        for rest in range(1, BIG):

            @pl.when(units - full * BIG == rest)
            def _(rest=rest, multiply=multiply, full=full):
                multiply(rest * unit * LANES)(full * (BIG * unit * LANES))

    if last:
        copies[0].wait()
        send_own_rows(outs, groups, rows, share, frame_ids, local[0])


def send_own_rows(outs, groups, rows, share, frame_ids, ky_ref):
    prods = outs[-1]
    width = groups * share
    group = lax.axis_index("frames")
    column = lax.broadcasted_iota(jnp.int32, (1, width), 1)
    parts = [
        jnp.where(column == dest * share + j, ky_ref[(group ^ dest) * share + j], 0)
        for dest in range(groups)
        for j in range(share)
    ]
    while len(parts) > 1:
        parts = [sum(parts[i : i + 2][1:], parts[i]) for i in range(0, len(parts), 2)]
    wanted = parts[0]
    ks = lax.broadcasted_iota(jnp.int32, (KMAX, width), 0) + 1
    hot = jnp.where(ks == wanted, 1.0, 0.0).astype(jnp.bfloat16)
    none = jnp.zeros_like(hot)
    hot = jnp.concatenate(
        [jnp.concatenate([hot, none], axis=1), jnp.concatenate([none, hot], axis=1)], axis=0
    )
    hot = jnp.concatenate([hot, hot, hot], axis=0)
    first_half = lax.broadcasted_iota(jnp.int32, (rows, 2 * KMAX), 1) < KMAX
    for place, frame in enumerate(frame_ids):
        top = prods[frame, 0:rows, :]
        low = pltpu.roll(prods[frame, rows : 2 * rows, :], KMAX, 1)
        terms = jnp.where(first_half, top - low, -(top + low))
        hi = terms.astype(jnp.bfloat16)
        rest = terms - hi.astype(jnp.float32)
        mid = rest.astype(jnp.bfloat16)
        tail = (rest - mid.astype(jnp.float32)).astype(jnp.bfloat16)
        split = jnp.concatenate([hi, mid, tail], axis=1)
        picked = lax.dot_general(
            hot, split, (((0,), (1,)), ((), ())), preferred_element_type=jnp.float32
        )
        for part in range(2):
            for dest in range(groups):
                at = part * width + dest * share
                to = (place * 2 + part) * share
                outs[dest][to : to + share, :] = picked[at : at + share, :]


def dft_table(table_ref, frames_total, atoms):
    weights = [0.5 - 0.5 * math.cos(2.0 * math.pi * (t + 0.5) / frames_total) for t in range(frames_total)]
    scale = 1.0 / math.sqrt(atoms * sum(w * w for w in weights))
    shape = (2 * frames_total, NW)
    row = lax.broadcasted_iota(jnp.int32, shape, 0)
    time = row // 2
    real = row % 2 == 0
    freq = lax.broadcasted_iota(jnp.int32, shape, 1)
    window = 0.5 - 0.5 * cis((time.astype(jnp.float32) + 0.5) / frames_total)[0]
    c, s = cis((time * freq % NW).astype(jnp.float32) / NW)
    cw, sw = scale * window * c, scale * window * s
    full = jnp.concatenate([jnp.where(real, cw, sw), jnp.where(real, -sw, cw)], axis=1)
    hi = full.astype(jnp.bfloat16)
    lo = (full - hi.astype(jnp.float32)).astype(jnp.bfloat16)
    none = jnp.zeros_like(hi)
    size = 2 * frames_total
    for split, part in enumerate((hi, lo, hi)):
        at = split * 2 * size
        table_ref[at : at + size, :] = jnp.concatenate([part, none], axis=1)
        table_ref[at + size : at + 2 * size, :] = jnp.concatenate([none, part], axis=1)


def spectrum_kernel(groups, frames_here, share, chunk, n_x, n_z, frames_total, atoms, *refs):
    srcs = refs[: groups * frames_here]
    out_hbm, out_ref, all_ref, table_ref, sem = refs[groups * frames_here :]
    block = srcs[0].shape[0]
    terms = frames_total * 2
    rows = n_x * n_z
    for frame in range(frames_here):
        for distance in range(groups):
            at = ((lax.axis_index("frames") ^ distance) * frames_here + frame) * block
            all_ref[pl.ds(pl.multiple_of(at, block), block), :] = srcs[frame * groups + distance][...]
    dft_table(table_ref, frames_total, atoms)

    copies = []
    for base in range(0, share, chunk):
        for first in range(base, base + chunk, 2 * PAIRS):
            stacks = []
            for j in range(first, first + 2 * PAIRS, 2):
                x = jnp.concatenate(
                    [all_ref[pl.ds(j + q, terms, stride=share), :] for q in range(2)], axis=0
                )
                hi = x.astype(jnp.bfloat16)
                lo = (x - hi.astype(jnp.float32)).astype(jnp.bfloat16)
                stacks.append(jnp.concatenate([hi, hi, lo], axis=0))
            y = lax.dot_general(
                jnp.concatenate(stacks, axis=1),
                table_ref[...],
                (((0,), (0,)), ((), ())),
                preferred_element_type=jnp.float32,
            )
            for q in range(2 * PAIRS):
                own = y[q // 2 * rows : (q // 2 + 1) * rows]
                at = q % 2 * 2 * NW
                re, im = own[:, at : at + NW], own[:, at + NW : at + 2 * NW]
                out_ref[:, first + q] = (re * re + im * im).reshape(n_x, n_z, NW)
        part = pl.ds(base, chunk)
        copies.append(
            pltpu.make_async_copy(
                out_ref.at[:, part], out_hbm.at[:, part], sem.at[base // chunk]
            )
        )
        copies[-1].start()
    for copy in copies:
        copy.wait()


def swap(value, axis, size, distance):
    return lax.ppermute(value, axis, [(i, i ^ distance) for i in range(size)])


def per_device(positions, counts, kvec_x, kvec_y, kvec_z):
    groups = lax.axis_size("frames")
    bricks = lax.axis_size("bricks")
    frames_here, capacity = positions.shape[1], positions.shape[2]
    n_x, n_z = kvec_x.shape[0] // bricks, kvec_z.shape[0]
    rows = n_x * n_z
    share = kvec_y.shape[0] // groups
    block = 2 * share
    vmem = pl.BlockSpec(memory_space=pltpu.VMEM)
    prods_shape = (frames_here, 2 * rows, 2 * KMAX)
    waves_shape = (n_x + n_z + 16, LANES)
    hbm = pl.BlockSpec(memory_space=pltpu.HBM)
    smem = pl.BlockSpec(memory_space=pltpu.SMEM)

    def density(shards, ids, sums, last, frame_ids=tuple(range(positions.shape[1]))):
        first = sums is None
        unit = UNIT if len(ids) > 2 else UNIT // 2
        lanes = -(-len(ids) * capacity // (BIG * unit * LANES)) * BIG * unit * LANES
        args = [counts, kvec_x, kvec_z, shards] if first else [kvec_y] if last else []
        args = [pltpu.with_memory_space_constraint(arg, pltpu.HBM) for arg in args]
        scratch = [pltpu.SMEM(arg.shape, jnp.int32) for arg in args[:3]]
        scratch += [
            pltpu.VMEM((2 * rows, lanes), jnp.bfloat16),
            pltpu.VMEM((2 * KMAX, lanes), jnp.bfloat16),
            pltpu.VMEM((unit * 2 * (n_x + 8) + 8, LANES), jnp.float32),
            pltpu.SemaphoreType.DMA((4,)),
        ]
        if last:
            out_shape = [jax.ShapeDtypeStruct((block, rows), jnp.float32)] * groups
            scratch = [pltpu.VMEM(prods_shape, jnp.float32)] + scratch
        else:
            out_shape = [jax.ShapeDtypeStruct(prods_shape, jnp.float32)]
            if first:
                out_shape.append(jax.ShapeDtypeStruct(waves_shape, jnp.float32))
                out_shape.append(jax.ShapeDtypeStruct(counts.shape, jnp.int32))
                out_shape.append(jax.ShapeDtypeStruct(shards.shape, jnp.float32))
        atoms = len(frame_ids) * len(ids) * capacity
        return pl.pallas_call(
            functools.partial(density_kernel, unit, frame_ids, ids, first, last, groups, n_x, n_z, share),
            out_shape=out_shape,
            in_specs=[hbm] * len(args) + ([] if first else [vmem] * 3 + [smem]),
            out_specs=[vmem, vmem, smem, vmem] if first else [vmem] * len(out_shape),
            scratch_shapes=scratch,
            cost_estimate=pl.CostEstimate(
                flops=atoms * rows * KMAX * 8, bytes_accessed=atoms * 12, transcendentals=0
            ),
            compiler_params=pltpu.CompilerParams(vmem_limit_bytes=48 << 20),
            name="density",
        )(*args, *([] if first else [shards, *sums]))

    held, fresh, ids = positions[None], positions[None], [0]
    new, sums, fixed = [0], None, None
    distance = bricks // 2
    while distance:
        got = swap(held, "bricks", bricks, distance)
        out = density(fresh, new, sums, False)
        if sums is None:
            fixed, held = out[1:3], out[3]
        got, prods = lax.optimization_barrier((got, out[0]))
        sums = (prods, *fixed)
        new = [i ^ distance for i in ids]
        ids, fresh = ids + new, got
        distance //= 2
        if distance:
            held = jnp.concatenate([held, got], axis=0)
    arrived = []
    for frame in range(frames_here):
        sends = density(got, new, sums, True, (frame,))
        got, sends, arrived = lax.optimization_barrier((got, sends, arrived))
        far = [swap(sends[d], "frames", groups, d) for d in range(1, groups)]
        arrived += [sends[0]] + far

    chunk = min(8, share)
    frames_total = frames_here * groups
    return pl.pallas_call(
        functools.partial(
            spectrum_kernel, groups, frames_here, share, chunk, n_x, n_z, frames_total, capacity * bricks
        ),
        out_shape=jax.ShapeDtypeStruct((n_x, share, n_z, NW), jnp.float32),
        in_specs=[vmem] * len(arrived),
        out_specs=hbm,
        scratch_shapes=[
            pltpu.VMEM((n_x, share, n_z, NW), jnp.float32),
            pltpu.VMEM((frames_total * block, rows), jnp.float32),
            pltpu.VMEM((12 * frames_total, 4 * NW), jnp.bfloat16),
            pltpu.SemaphoreType.DMA((share // chunk,)),
        ],
        compiler_params=pltpu.CompilerParams(vmem_limit_bytes=16 << 20),
        name="spectrum",
    )(*arrived)


def solution(mesh):
    return jax.shard_map(
        per_device,
        mesh=mesh,
        in_specs=(P(None, "frames", "bricks"), P("frames", None), P(), P(), P()),
        out_specs=P("bricks", "frames", None, None),
        check_vma=False,
    )
```

```python
import functools
import math

import jax
import jax.numpy as jnp
import numpy as np
from jax import lax
from jax.experimental import pallas as pl
from jax.experimental.pallas import tpu as pltpu
from jax.sharding import PartitionSpec as P

NW = 128
KMAX = 64
LANES = 128
UNIT = 4
PAIRS = 2
BIG = 8

def _fit(fun, degree):
    nodes = 0.125 * (1.0 + np.cos(np.pi * (np.arange(64) + 0.5) / 64))
    series = np.polynomial.chebyshev.Chebyshev.fit(nodes, fun(np.sqrt(nodes)), degree, domain=[0.0, 0.25])
    return [float(c) for c in series.convert(kind=np.polynomial.Polynomial).coef]


COS_C = _fit(lambda f: math.sqrt(2.0) * np.cos(np.pi * f), 4)
SIN_C = _fit(lambda f: math.sqrt(2.0) * np.sin(np.pi * f) / f, 4)


def _poly(coefs, u):
    acc = coefs[-1] * u + coefs[-2]
    for c in coefs[-3::-1]:
        acc = acc * u + c
    return acc


def cis(turns):
    f = turns - jnp.round(turns)
    u = f * f
    half_c = _poly(COS_C, u)
    half_s = _poly(SIN_C, u) * f
    return 1.0 - half_s * half_s, half_s * half_c


def density_kernel(unit, ids, first, last, groups, n_x, n_z, share, *refs):
    n_args = 4 if first else 1 if last else 0
    args, refs = refs[:n_args], refs[n_args:]
    left_ref, right_ref, row_ref, arg_sem = refs[-4:]
    refs = refs[:-4]
    if not first:
        (pos_ref, prod_in, kb_ref, counts_ref), refs = refs[:4], refs[4:]
    n_local = min(n_args, 3)
    outs, local = refs[: len(refs) - n_local], refs[len(refs) - n_local :]
    if first:
        local = (*local, outs[3])
    copies = [
        pltpu.make_async_copy(args[i], local[i], arg_sem.at[i]) for i in range(n_args)
    ]
    for copy in copies:
        copy.start()
    if first:
        counts_ref, pos_ref, kb_ref = local[0], local[3], outs[1]
    rows = n_x * n_z
    n_shards, _, frames_here, capacity = pos_ref.shape
    brick = lax.axis_index("bricks")
    lane = lax.broadcasted_iota(jnp.int32, (n_z, LANES), 1)

    if first:
        kx_ref, kz_ref = local[1:3]
        copies[0].wait()
        for frame in range(frames_here):
            for at in range(counts_ref.shape[1]):
                outs[2][frame, at] = counts_ref[frame, at]
        copies[1].wait()
        copies[2].wait()
        for row in range(n_x + n_z + 16):
            if row < n_x:
                k = kx_ref[brick * n_x + row].astype(jnp.float32)
            elif row < n_x + n_z:
                k = kz_ref[row - n_x].astype(jnp.float32)
            else:
                q = row - n_x - n_z
                k = float(q + 1 if q < 8 else 8 * (q - 7))
            kb_ref[row : row + 1, :] = jnp.full((1, LANES), k, jnp.float32)
        copies[3].wait()

    for frame in range(frames_here):
        counts = [counts_ref[frame, brick ^ d] for d in ids]
        starts = [jnp.int32(0)]
        for count in counts:
            starts.append(starts[-1] + (count + LANES - 1) // LANES)

        def build(item, slot, frame=frame, counts=counts, starts=starts):
            shard, start, count = jnp.int32(0), starts[0], counts[0]
            for s in range(1, n_shards):
                later = item >= starts[s]
                shard = jnp.where(later, s, shard)
                start = jnp.where(later, starts[s], start)
                count = jnp.where(later, counts[s], count)
            offset = (item - start) * LANES
            where = pl.ds(pl.multiple_of(jnp.minimum(offset, capacity - LANES), LANES), LANES)
            x = pos_ref[shard, 0, pl.ds(frame, 1), where]
            y = pos_ref[shard, 1, pl.ds(frame, 1), where]
            z = pos_ref[shard, 2, pl.ds(frame, 1), where]
            cx, sx = cis(kb_ref[0:n_x, :] * x)
            cz, sz = cis(kb_ref[n_x : n_x + n_z, :] * z)
            cy, sy = cis(kb_ref[n_x + n_z : n_x + n_z + 16, :] * y)
            live = lane + offset < count
            cz = jnp.where(live, cz, 0.0)
            sz = jnp.where(live, sz, 0.0)
            to = pl.ds(pl.multiple_of(item * LANES, LANES), LANES)
            half = n_x + 8
            base = slot * 2 * half
            row_ref[base : base + half, :] = jnp.concatenate([cx, cy[8:16]], axis=0)
            row_ref[base + half : base + 2 * half, :] = jnp.concatenate([sx, sy[8:16]], axis=0)

            def spread(q):
                return (
                    row_ref[pl.ds(base + q, 8, stride=0), :],
                    row_ref[pl.ds(base + half + q, 8, stride=0), :],
                )

            for i in range(0, n_x, 2):
                re, im = [], []
                for q in (i, i + 1):
                    a, b = spread(q)
                    re.append(a * cz - b * sz)
                    im.append(b * cz + a * sz)
                at = i * n_z
                left_ref[at : at + 2 * n_z, to] = jnp.concatenate(re, axis=0).astype(jnp.bfloat16)
                at += rows
                left_ref[at : at + 2 * n_z, to] = jnp.concatenate(im, axis=0).astype(jnp.bfloat16)
            ce, se = cy[0:8], sy[0:8]
            re, im = [ce], [se]
            for q in range(7):
                a, b = spread(n_x + q)
                re.append(a * ce - b * se)
                im.append(b * ce + a * se)
            for q in range(0, 8, 2):
                right_ref[8 * q : 8 * q + 16, to] = jnp.concatenate(re[q : q + 2], axis=0).astype(jnp.bfloat16)
                right_ref[KMAX + 8 * q : KMAX + 8 * q + 16, to] = jnp.concatenate(im[q : q + 2], axis=0).astype(jnp.bfloat16)

        def build_unit(at_unit, carry, build=build):
            for g in range(unit):
                build(at_unit * unit + g, g)
            return carry

        units = (starts[-1] + unit - 1) // unit
        lax.fori_loop(0, units, build_unit, 0)
        prod_ref = outs[0].at[frame] if not last else outs[-1].at[frame]
        prod_ref[...] = jnp.zeros(prod_ref.shape, jnp.float32) if first else prod_in[frame]

        def multiply(width):
            def step(base):
                where = pl.ds(pl.multiple_of(base, unit * LANES), width)
                prod_ref[...] += lax.dot_general(
                    left_ref[:, where],
                    right_ref[:, where],
                    (((1,), (1,)), ((), ())),
                    preferred_element_type=jnp.float32,
                )

            return step

        wide = multiply(BIG * unit * LANES)
        full = units // BIG

        def wide_step(i, carry, wide=wide):
            wide(i * (BIG * unit * LANES))
            return carry

        lax.fori_loop(0, full, wide_step, 0)
        for rest in range(1, BIG):

            @pl.when(units - full * BIG == rest)
            def _(rest=rest, multiply=multiply, full=full):
                multiply(rest * unit * LANES)(full * (BIG * unit * LANES))

    if last:
        copies[0].wait()
        send_own_rows(outs, groups, rows, share, frames_here, local[0])


def send_own_rows(outs, groups, rows, share, frames_here, ky_ref):
    prods = outs[-1]
    width = groups * share
    group = lax.axis_index("frames")
    column = lax.broadcasted_iota(jnp.int32, (1, width), 1)
    parts = [
        jnp.where(column == dest * share + j, ky_ref[(group ^ dest) * share + j], 0)
        for dest in range(groups)
        for j in range(share)
    ]
    while len(parts) > 1:
        parts = [sum(parts[i : i + 2][1:], parts[i]) for i in range(0, len(parts), 2)]
    wanted = parts[0]
    ks = lax.broadcasted_iota(jnp.int32, (KMAX, width), 0) + 1
    hot = jnp.where(ks == wanted, 1.0, 0.0).astype(jnp.bfloat16)
    none = jnp.zeros_like(hot)
    hot = jnp.concatenate(
        [jnp.concatenate([hot, none], axis=1), jnp.concatenate([none, hot], axis=1)], axis=0
    )
    hot = jnp.concatenate([hot, hot, hot], axis=0)
    first_half = lax.broadcasted_iota(jnp.int32, (rows, 2 * KMAX), 1) < KMAX
    for frame in range(frames_here):
        top = prods[frame, 0:rows, :]
        low = pltpu.roll(prods[frame, rows : 2 * rows, :], KMAX, 1)
        terms = jnp.where(first_half, top - low, -(top + low))
        hi = terms.astype(jnp.bfloat16)
        rest = terms - hi.astype(jnp.float32)
        mid = rest.astype(jnp.bfloat16)
        tail = (rest - mid.astype(jnp.float32)).astype(jnp.bfloat16)
        split = jnp.concatenate([hi, mid, tail], axis=1)
        picked = lax.dot_general(
            hot, split, (((0,), (1,)), ((), ())), preferred_element_type=jnp.float32
        )
        for part in range(2):
            for dest in range(groups):
                at = part * width + dest * share
                to = (frame * 2 + part) * share
                outs[dest][to : to + share, :] = picked[at : at + share, :]


def dft_table(frames_total, atoms, after_ref, table_ref):
    weights = [0.5 - 0.5 * math.cos(2.0 * math.pi * (t + 0.5) / frames_total) for t in range(frames_total)]
    scale = 1.0 / math.sqrt(atoms * sum(w * w for w in weights))
    shape = (2 * frames_total, NW)
    row = lax.broadcasted_iota(jnp.int32, shape, 0)
    time = row // 2
    real = row % 2 == 0
    freq = lax.broadcasted_iota(jnp.int32, shape, 1)
    window = 0.5 - 0.5 * cis((time.astype(jnp.float32) + 0.5) / frames_total)[0]
    c, s = cis((time * freq % NW).astype(jnp.float32) / NW)
    cw, sw = scale * window * c, scale * window * s
    full = jnp.concatenate([jnp.where(real, cw, sw), jnp.where(real, -sw, cw)], axis=1)
    hi = full.astype(jnp.bfloat16)
    lo = (full - hi.astype(jnp.float32)).astype(jnp.bfloat16)
    none = jnp.zeros_like(hi)
    size = 2 * frames_total
    for split, part in enumerate((hi, lo, hi)):
        at = split * 2 * size
        table_ref[at : at + size, :] = jnp.concatenate([part, none], axis=1)
        table_ref[at + size : at + 2 * size, :] = jnp.concatenate([none, part], axis=1)


def spectrum_kernel(groups, share, chunk, n_x, n_z, *refs):
    srcs = refs[:groups]
    table_ref, out_hbm, out_ref, all_ref, sem = refs[groups:]
    block = srcs[0].shape[0]
    terms = groups * block // share
    rows = n_x * n_z
    for distance in range(groups):
        at = pl.multiple_of((lax.axis_index("frames") ^ distance) * block, block)
        all_ref[pl.ds(at, block), :] = srcs[distance][...]
    copies = []
    for base in range(0, share, chunk):
        for first in range(base, base + chunk, 2 * PAIRS):
            stacks = []
            for j in range(first, first + 2 * PAIRS, 2):
                x = jnp.concatenate(
                    [all_ref[pl.ds(j + q, terms, stride=share), :] for q in range(2)], axis=0
                )
                hi = x.astype(jnp.bfloat16)
                lo = (x - hi.astype(jnp.float32)).astype(jnp.bfloat16)
                stacks.append(jnp.concatenate([hi, hi, lo], axis=0))
            y = lax.dot_general(
                jnp.concatenate(stacks, axis=1),
                table_ref[...],
                (((0,), (0,)), ((), ())),
                preferred_element_type=jnp.float32,
            )
            for q in range(2 * PAIRS):
                own = y[q // 2 * rows : (q // 2 + 1) * rows]
                at = q % 2 * 2 * NW
                re, im = own[:, at : at + NW], own[:, at + NW : at + 2 * NW]
                out_ref[:, first + q] = (re * re + im * im).reshape(n_x, n_z, NW)
        part = pl.ds(base, chunk)
        copies.append(
            pltpu.make_async_copy(
                out_ref.at[:, part], out_hbm.at[:, part], sem.at[base // chunk]
            )
        )
        copies[-1].start()
    for copy in copies:
        copy.wait()


def swap(value, axis, size, distance):
    return lax.ppermute(value, axis, [(i, i ^ distance) for i in range(size)])


def per_device(positions, counts, kvec_x, kvec_y, kvec_z):
    groups = lax.axis_size("frames")
    bricks = lax.axis_size("bricks")
    frames_here, capacity = positions.shape[1], positions.shape[2]
    n_x, n_z = kvec_x.shape[0] // bricks, kvec_z.shape[0]
    rows = n_x * n_z
    share = kvec_y.shape[0] // groups
    block = frames_here * 2 * share
    vmem = pl.BlockSpec(memory_space=pltpu.VMEM)
    prods_shape = (frames_here, 2 * rows, 2 * KMAX)
    waves_shape = (n_x + n_z + 16, LANES)
    hbm = pl.BlockSpec(memory_space=pltpu.HBM)
    smem = pl.BlockSpec(memory_space=pltpu.SMEM)

    def density(shards, ids, sums, last):
        first = sums is None
        unit = UNIT if len(ids) > 2 else UNIT // 2
        lanes = -(-len(ids) * capacity // (BIG * unit * LANES)) * BIG * unit * LANES
        args = [counts, kvec_x, kvec_z, shards] if first else [kvec_y] if last else []
        args = [pltpu.with_memory_space_constraint(arg, pltpu.HBM) for arg in args]
        scratch = [pltpu.SMEM(arg.shape, jnp.int32) for arg in args[:3]]
        scratch += [
            pltpu.VMEM((2 * rows, lanes), jnp.bfloat16),
            pltpu.VMEM((2 * KMAX, lanes), jnp.bfloat16),
            pltpu.VMEM((unit * 2 * (n_x + 8) + 8, LANES), jnp.float32),
            pltpu.SemaphoreType.DMA((4,)),
        ]
        if last:
            out_shape = [jax.ShapeDtypeStruct((block, rows), jnp.float32)] * groups
            scratch = [pltpu.VMEM(prods_shape, jnp.float32)] + scratch
        else:
            out_shape = [jax.ShapeDtypeStruct(prods_shape, jnp.float32)]
            if first:
                out_shape.append(jax.ShapeDtypeStruct(waves_shape, jnp.float32))
                out_shape.append(jax.ShapeDtypeStruct(counts.shape, jnp.int32))
                out_shape.append(jax.ShapeDtypeStruct(shards.shape, jnp.float32))
        atoms = frames_here * len(ids) * capacity
        return pl.pallas_call(
            functools.partial(density_kernel, unit, ids, first, last, groups, n_x, n_z, share),
            out_shape=out_shape,
            in_specs=[hbm] * len(args) + ([] if first else [vmem] * 3 + [smem]),
            out_specs=[vmem, vmem, smem, vmem] if first else [vmem] * len(out_shape),
            scratch_shapes=scratch,
            cost_estimate=pl.CostEstimate(
                flops=atoms * rows * KMAX * 8, bytes_accessed=atoms * 12, transcendentals=0
            ),
            compiler_params=pltpu.CompilerParams(vmem_limit_bytes=48 << 20),
            name="density",
        )(*args, *([] if first else [shards, *sums]))

    held, fresh, ids = positions[None], positions[None], [0]
    new, sums, fixed = [0], None, None
    distance = bricks // 2
    while distance:
        got = swap(held, "bricks", bricks, distance)
        out = density(fresh, new, sums, False)
        if sums is None:
            fixed, held = out[1:3], out[3]
        got, prods = lax.optimization_barrier((got, out[0]))
        sums = (prods, *fixed)
        new = [i ^ distance for i in ids]
        ids, fresh = ids + new, got
        distance //= 2
        if distance:
            held = jnp.concatenate([held, got], axis=0)
    sends = density(fresh, new, sums, True)
    far = [swap(sends[d], "frames", groups, d) for d in range(groups - 1, 0, -1)]
    got = [sends[0]] + far[::-1]

    chunk = min(8, share)
    frames_total = frames_here * groups
    table = pl.pallas_call(
        functools.partial(dft_table, frames_total, capacity * bricks),
        out_shape=jax.ShapeDtypeStruct((12 * frames_total, 4 * NW), jnp.bfloat16),
        in_specs=[pl.BlockSpec(memory_space=pl.ANY)],
        out_specs=vmem,
        compiler_params=pltpu.CompilerParams(vmem_limit_bytes=16 << 20),
        name="table",
    )(sends[0])
    return pl.pallas_call(
        functools.partial(spectrum_kernel, groups, share, chunk, n_x, n_z),
        out_shape=jax.ShapeDtypeStruct((n_x, share, n_z, NW), jnp.float32),
        in_specs=[vmem] * (groups + 1),
        out_specs=hbm,
        scratch_shapes=[
            pltpu.VMEM((n_x, share, n_z, NW), jnp.float32),
            pltpu.VMEM((groups * block, rows), jnp.float32),
            pltpu.SemaphoreType.DMA((share // chunk,)),
        ],
        compiler_params=pltpu.CompilerParams(vmem_limit_bytes=16 << 20),
        name="spectrum",
    )(*got, table)


def solution(mesh):
    return jax.shard_map(
        per_device,
        mesh=mesh,
        in_specs=(P(None, "frames", "bricks"), P("frames", None), P(), P(), P()),
        out_specs=P("bricks", "frames", None, None),
        check_vma=False,
    )
```
